128 devices in a mesh: req: 16 (over z, y), tp: 8 (over x, core).
Axes of the slice: x: 4, y: 4, z: 4, core: 2. Of those that a mesh axis runs over, the one named last changes fastest.
Arguments:
- new_hidden: bfloat16 [256, 2, 7168], P('req'), may hold values from -6 to 6
- norm_gain: float32 [7168], replicated, may hold values from 0.25 to 1.75
- w_query: bfloat16 [7168, 7168], P(None, 'tp'), may hold values from -8 to 8
- w_key: bfloat16 [7168, 1024], P(None, 'tp'), may hold values from -8 to 8
- w_value: bfloat16 [7168, 1024], P(None, 'tp'), may hold values from -0.0625 to 0.0625
- hidden_store: bfloat16 [16, 409, 7168], P('req'), may hold values from -6 to 6
- key_cache: bfloat16 [16, 4096, 1024], P('req', None, 'tp'), may hold values from -16 to 16
- value_cache: bfloat16 [16, 4096, 1024], P('req', None, 'tp'), may hold values from -6 to 6
- tail_keys: bfloat16 [256, 256, 1024], P('req', None, 'tp'), may hold values from -16 to 16
- tail_values: bfloat16 [256, 256, 1024], P('req', None, 'tp'), may hold values from -6 to 6
- prompt_len: int32 [16], replicated, may hold values from 512 to 4096
- tail_len: int32 [256], P('req'), may hold values from 1 to 256
- recomp_pos: int32 [16, 409], P('req'), may hold values from 0 to 4089, as said below
- cont_prompt: int32 [256, 1], replicated, may hold values from 0 to 15; in each aligned block of 16 rows (0 to 15, 16 to 31, ...) at most 2 rows name the same one
- score_weight: float32 [7168], P('tp'), may hold values from -1.2 to 1.2
Outputs:
- attended: bfloat16 [256, 2, 7168], P('req', None, 'tp')
- scores: float32 [256], P('req')
The draws below stay inside these ranges and needn't reach their ends.
Inputs may be any that keep to these rules, and one draw needn't show every extreme that they name: recomp_pos[p, j] lies in [10 j, 10 j + 9]. `cont_prompt`: within the rows of one device (aligned blocks of 16 continuations), no prompt is named by more than 2 continuations.
All inputs are finite; a program needn't handle non-finite values.
Results may differ from the reference program's by a relative error of at most 0.0156.
The reference program's roundings to bfloat16 on the way count: a program that leaves them out, or rounds other values in their place, can miss the bound.
Values may be sent and summed in bfloat16 or wider, within the bound.
A program may use at most 192 MiB of HBM per device.

```python
import math
import jax
import jax.numpy as jnp
import numpy as np
from jax import lax

D = 7168
HEADS = 56
KVH = 8
HD = 128
CTX = 4096
TAIL = 256
CONT_DEV = 16
MOST = 2
STRIDE = 10
RECOMP = 409
NPROMPT = 16
CONTS = 256


def cache_keys(key, shape):
    return jnp.clip(jax.random.normal(key, shape, jnp.float32) * 2.5, -15.0, 15.0).astype(jnp.bfloat16)


def bounded_counts(key, count, lowest, highest):
    counts = jax.random.randint(key, (count,), lowest, highest + 1)
    order = jax.random.permutation(jax.random.fold_in(key, 3), count)
    return counts.at[order[0]].set(highest).at[order[1]].set(lowest).astype(jnp.int32)


def draw_w_query(key, part):
    inner = jax.random.fold_in(key, 31)
    entries = jnp.clip(jax.random.normal(inner, (D, HEADS * HD), jnp.float32), -6.0, 6.0)
    return (entries * D ** (-0.5)).astype(jnp.bfloat16)


def draw_w_key(key, part):
    inner = jax.random.fold_in(key, 32)
    entries = jnp.clip(jax.random.normal(inner, (D, KVH * HD), jnp.float32), -6.0, 6.0)
    return (entries * 2.5 * D ** (-0.5)).astype(jnp.bfloat16)


def draw_key_cache(key, part):
    return cache_keys(jax.random.fold_in(key, 21), (NPROMPT, CTX, KVH * HD))


def draw_tail_keys(key, part):
    return cache_keys(jax.random.fold_in(key, 22), (CONTS, TAIL, KVH * HD))


def draw_prompt_len(key, part):
    return bounded_counts(jax.random.fold_in(key, 23), NPROMPT, CTX // 8, CTX)


def draw_tail_len(key, part):
    return bounded_counts(jax.random.fold_in(key, 24), CONTS, 1, TAIL)


def draw_recomp_pos(key, part):
    inner = jax.random.fold_in(key, 25)
    offsets = jax.random.randint(inner, (NPROMPT, RECOMP), 0, STRIDE)
    chosen = jax.random.randint(jax.random.fold_in(inner, 5), (2,), 0, NPROMPT)
    offsets = offsets.at[chosen[0], RECOMP - 1].set(STRIDE - 1).at[chosen[1], 0].set(0)
    return (jnp.arange(RECOMP, dtype=jnp.int32)[None, :] * STRIDE + offsets).astype(jnp.int32)


def block_levels(stream_key, extent, cuts, low, top_value):
    def one(axis_at, parts):
        draws = jax.random.uniform(jax.random.fold_in(jax.random.fold_in(stream_key, 6), axis_at), (parts,), jnp.float32, low / len(cuts), top_value / len(cuts))
        return jnp.repeat(jnp.exp(draws), extent[axis_at] // parts).reshape((-1,) + (1,) * (len(extent) - axis_at - 1))

    loudness = one(*cuts[0])
    for cut in cuts[1:]:
        loudness = loudness * one(*cut)
    return loudness


def routed_block(own_key, own, number, rows, number_of, top, reach, slope):
    order = jax.random.permutation(own_key, number_of)
    packed, ordinary = portions_of(number_of, rows * top, reach, slope, True), portions_of(number_of, rows * top, reach, slope, False)
    places = jnp.arange(number_of)

    def named(sizes, turn):
        used = int((sizes > 0).sum())
        fixed = max(1, used // 4)
        shifted = fixed + (places - fixed + turn * (used - fixed)) % max(1, number_of - fixed)
        return jnp.zeros((number_of,), jnp.int32).at[order[jnp.where(places < fixed, places, shifted)]].set(jnp.asarray(sizes, jnp.int32))

    sizes = jnp.where(number % 4 == 0, named(packed, number // 4), named(ordinary, number - number // 4 - 1))
    mixed = jax.random.permutation(jax.random.fold_in(own, 3), number_of)
    donor, taker = mixed[0:number_of // 2 * 2:2], mixed[1:number_of // 2 * 2:2]
    room = jnp.minimum(sizes[donor] - 1, reach - sizes[taker]) // 2
    room = jnp.where((donor == order[0]) | (taker == order[0]) | (sizes[taker] == 0), 0, jnp.maximum(room, 0))
    shifted = jax.random.randint(jax.random.fold_in(own, 4), (number_of // 2,), 0, 1 << 20) % (room + 1)
    sizes = sizes.at[donor].add(-shifted).at[taker].add(shifted)
    items = jnp.searchsorted(jnp.cumsum(sizes), jnp.arange(rows * top), side="right").astype(jnp.int32)
    table = items.reshape(top, rows).T
    table = table[jax.random.permutation(jax.random.fold_in(own, 1), rows)]
    turn = jax.random.randint(jax.random.fold_in(own, 2), (rows, 1), 0, top)
    return jnp.take_along_axis(table, (jnp.arange(top)[None, :] + turn) % top, axis=1)


def portions_of(number_of, total, bound, lean, full):
    weights = [(1 << 20) // math.isqrt(rank ** lean) + 1 for rank in range(1, number_of + 1)]
    largest = bound if full else min(bound, max(-(-total // number_of), total * weights[0] // sum(weights)))
    least = 1 if total - largest >= number_of - 1 else 0
    given, surplus = [largest] + [least] * (number_of - 1), total - largest - least * (number_of - 1)
    while surplus > 0:
        candidates = [i for i in range(1, number_of) if given[i] < largest] or [i for i in range(1, number_of) if given[i] < bound]
        whole, remaining = sum([weights[i] for i in candidates]), surplus
        for i in candidates:
            more = min(bound - given[i], max(1, remaining * weights[i] // whole), surplus)
            given[i] = given[i] + more
            surplus = surplus - more
    return np.array(given)


def noise(stream_key, extent, spread, reach, cuts=(), kind=jnp.bfloat16):
    values = jax.random.normal(stream_key, extent, jnp.float32) * spread
    if len(cuts) > 0:
        values = block_levels(stream_key, extent, cuts, -0.22, 0.18) * values
    return jnp.clip(values, min=-reach, max=reach).astype(kind)


def setup_inputs(seed: int = 0) -> dict:
    key_of = jax.random.split(jax.random.key(seed), 16)
    new_hidden = noise(key_of[0], (CONTS, 2, D), 1.0, 6.0, ((0, 16),))
    norm_gain = jnp.clip(1.0 + 0.15 * jax.random.normal(key_of[1], (D,), jnp.float32), 0.25, 1.75)
    w_query = draw_w_query(jax.random.fold_in(key_of[15], 71), 0)
    w_key = draw_w_key(jax.random.fold_in(key_of[15], 71), 0)
    w_value = noise(key_of[4], (D, KVH * HD), D ** -0.5, 0.0625, ((1, 8),))
    hidden_store = noise(key_of[5], (NPROMPT, RECOMP, D), 1.0, 6.0, ((0, 16),))
    key_cache = draw_key_cache(jax.random.fold_in(key_of[15], 71), 0)
    value_cache = noise(key_of[7], (NPROMPT, CTX, KVH * HD), 1.0, 6.0, ((0, 16), (2, 8)))
    tail_keys = draw_tail_keys(jax.random.fold_in(key_of[15], 71), 0)
    tail_values = noise(key_of[9], (CONTS, TAIL, KVH * HD), 1.0, 6.0, ((0, 16), (2, 8)))
    prompt_len = draw_prompt_len(jax.random.fold_in(key_of[15], 71), 0)
    tail_len = draw_tail_len(jax.random.fold_in(key_of[15], 71), 0)
    recomp_pos = draw_recomp_pos(jax.random.fold_in(key_of[15], 71), 0)
    cont_prompt_keys = jax.random.split(jax.random.fold_in(key_of[13], 1), CONTS // CONT_DEV)
    cont_prompt_turns = jax.random.permutation(jax.random.fold_in(key_of[13], 3), CONTS // CONT_DEV)
    cont_prompt = jax.vmap(lambda own, number: routed_block(jax.random.fold_in(key_of[13], 2), own, number, CONT_DEV, NPROMPT, 1, MOST, 1))(cont_prompt_keys, cont_prompt_turns).reshape((CONTS, 1))
    score_weight = noise(key_of[14], (HEADS * HD,), 0.2, 1.2, ((0, 8),), jnp.float32)
    return {"new_hidden": new_hidden, "norm_gain": norm_gain, "w_query": w_query, "w_key": w_key, "w_value": w_value, "hidden_store": hidden_store, "key_cache": key_cache, "value_cache": value_cache, "tail_keys": tail_keys, "tail_values": tail_values, "prompt_len": prompt_len, "tail_len": tail_len, "recomp_pos": recomp_pos, "cont_prompt": cont_prompt, "score_weight": score_weight}


rope_base = 5000000.0

def norm_rows(values, gain):
    widened = values.astype(jnp.float32)
    square = lax.optimization_barrier(jnp.mean(widened * widened, axis=-1, keepdims=True))
    return (widened * lax.rsqrt(square + 1e-05) * gain).astype(jnp.bfloat16)

def rotate(vector, where_at):
    half = vector.shape[-1] // 2
    freq = rope_base ** (-2.0 * jnp.arange(half, dtype=jnp.float32) / vector.shape[-1])
    angle = where_at.astype(jnp.float32)[..., None] * freq
    first = vector[..., :half]
    second = vector[..., half:]
    return jnp.concatenate([first * jnp.cos(angle) - second * jnp.sin(angle), second * jnp.cos(angle) + first * jnp.sin(angle)], axis=-1)

def set_terms(scores, mask, values, form):
    masked = jnp.where(mask, scores, -1e+30)
    top = lax.optimization_barrier(jnp.max(masked, axis=-1))
    weights = jnp.where(mask, jnp.exp(masked - top[..., None]), 0.0).astype(jnp.bfloat16)
    total = lax.optimization_barrier(jnp.sum(weights.astype(jnp.float32), axis=-1))
    out = jnp.einsum(form, weights.astype(jnp.float32), values.astype(jnp.float32))
    return (top, total, out)

def reference(new_hidden, norm_gain, w_query, w_key, w_value, hidden_store, key_cache, value_cache, tail_keys, tail_values, prompt_len, tail_len, recomp_pos, cont_prompt, score_weight):
    cont_prompt = cont_prompt.reshape(-1)
    group = HEADS // KVH
    scale = HD ** (-0.5)
    normed = norm_rows(new_hidden, norm_gain).reshape(CONTS * 2, D)
    position = (prompt_len[cont_prompt] + tail_len)[:, None] + jnp.arange(2, dtype=jnp.int32)[None, :]
    query = rotate(jnp.dot(normed, w_query, preferred_element_type=jnp.float32).reshape(CONTS, 2, HEADS, HD), position[..., None]).astype(jnp.bfloat16)
    key_new = rotate(jnp.dot(normed, w_key, preferred_element_type=jnp.float32).reshape(CONTS, 2, KVH, HD), position[..., None]).astype(jnp.bfloat16)
    value_new = jnp.dot(normed, w_value, preferred_element_type=jnp.float32).astype(jnp.bfloat16).reshape(CONTS, 2, KVH, HD)
    stored = norm_rows(hidden_store, norm_gain).reshape(NPROMPT * RECOMP, D)
    key_re = rotate(jnp.dot(stored, w_key, preferred_element_type=jnp.float32).reshape(NPROMPT, RECOMP, KVH, HD), recomp_pos[..., None]).astype(jnp.bfloat16).reshape(NPROMPT, RECOMP, KVH * HD)
    value_re = jnp.dot(stored, w_value, preferred_element_type=jnp.float32).astype(jnp.bfloat16).reshape(NPROMPT, RECOMP, KVH * HD)
    prompt_rows = jnp.arange(NPROMPT, dtype=jnp.int32)[:, None]
    key_fixed = key_cache.at[prompt_rows, recomp_pos].set(key_re)
    value_fixed = value_cache.at[prompt_rows, recomp_pos].set(value_re)
    ctx_range = jnp.arange(CTX, dtype=jnp.int32)
    tail_range = jnp.arange(TAIL, dtype=jnp.int32)
    new_mask = (jnp.arange(2)[None, :] <= jnp.arange(2)[:, None])[:, None, None, :]

    def one_cont(item):
        query_one, key_one, value_one, tail_k, tail_v, tail_count, prompt = item
        grouped = query_one.reshape(2, KVH, group, HD).astype(jnp.float32)
        keys = key_fixed[prompt].reshape(CTX, KVH, HD).astype(jnp.float32)
        prefix_s = jnp.einsum('tkgd,nkd->tkgn', grouped, keys) * scale
        prefix = set_terms(prefix_s, (ctx_range < prompt_len[prompt])[None, None, None, :], value_fixed[prompt].reshape(CTX, KVH, HD), 'tkgn,nkd->tkgd')
        tail_s = jnp.einsum('tkgd,nkd->tkgn', grouped, tail_k.reshape(TAIL, KVH, HD).astype(jnp.float32)) * scale
        tail = set_terms(tail_s, (tail_range < tail_count)[None, None, None, :], tail_v.reshape(TAIL, KVH, HD), 'tkgn,nkd->tkgd')
        new_s = jnp.einsum('tkgd,skd->tkgs', grouped, key_one.astype(jnp.float32)) * scale
        fresh = set_terms(new_s, new_mask, value_one, 'tkgs,skd->tkgd')
        highest = jnp.maximum(jnp.maximum(prefix[0], tail[0]), fresh[0])
        numer = jnp.zeros((2, KVH, group, HD), jnp.float32)
        denom = jnp.zeros((2, KVH, group), jnp.float32)
        for part in (prefix, tail, fresh):
            factor = jnp.exp(part[0] - highest)
            numer = numer + factor[..., None] * part[2]
            denom = denom + factor * part[1]
        return (numer / denom[..., None]).astype(jnp.bfloat16).reshape(2, HEADS * HD)
    attended = lax.map(one_cont, (query, key_new, value_new, tail_keys, tail_values, tail_len, cont_prompt))
    scores = lax.optimization_barrier(jnp.sum(attended[:, 1, :].astype(jnp.float32) * score_weight, axis=-1))
    return (attended, scores)
```

```python
import functools
import math

import jax
import jax.numpy as jnp
import numpy as np
from jax import lax
from jax.experimental import pallas as pl
from jax.experimental.pallas import tpu as pltpu
from jax.sharding import PartitionSpec as P

MESH = pl.DeviceIdType.MESH
HD = 128
NEG = -1e30
THETA = 5000000.0
LOG2E = math.log2(math.e)
F32 = jnp.float32
BF16 = jnp.bfloat16
I32 = jnp.int32


def iota(shape, dim):
    return lax.broadcasted_iota(I32, shape, dim)


def dot(a, b):
    return jnp.dot(a, b, preferred_element_type=F32)


def dot_t(a, b):
    return lax.dot_general(a, b, (((1,), (1,)), ((), ())), preferred_element_type=F32)


def onehot(mask):
    return jnp.where(mask, 1.0, 0.0).astype(BF16)


def kernel(
    dims,
    nh_hbm,
    gain_ref,
    wq_hbm,
    wk_hbm,
    wv_hbm,
    hs_hbm,
    kc_hbm,
    vc_hbm,
    tk_hbm,
    tv_hbm,
    plen_ref,
    tlen_ref,
    rpos_ref,
    cont_ref,
    sw_ref,
    freq_ref,
    out_ref,
    score_ref,
    nh,
    wq,
    w,
    hs,
    sn,
    kk,
    vv,
    tk,
    tv,
    pos_row,
    posb,
    ropec,
    ropes,
    bias,
    qacc,
    kvacc,
    qs,
    qt,
    xs,
    rq,
    s_buf,
    rs,
    rr,
    st,
    to,
    scs,
    scr,
    in_sem,
    wq_sem,
    qsend,
    qrecv,
    rsend,
    rrecv,
    ssend,
    srecv,
):
    n_req, n_tp, inner, D, CTX, TAIL, RECOMP, CD, G = dims
    T = 2
    ROWS = CD * T
    RP = -(-RECOMP // 32) * 32
    KT = kk.shape[0]
    outer = n_req // inner
    me = lax.axis_index("req")
    mt = lax.axis_index("tp")
    scale = HD ** (-0.5) * LOG2E
    CH = wq.shape[1]
    n_ch = wq.shape[0]

    load_nh = pltpu.make_async_copy(nh_hbm, nh, in_sem.at[0])
    load_nh.start()
    loads_q = [
        pltpu.make_async_copy(wq_hbm.at[pl.ds(i * CH, CH)], wq.at[i], wq_sem.at[i])
        for i in range(n_ch)
    ]
    for copy in loads_q:
        copy.start()
    load_wk = pltpu.make_async_copy(wk_hbm, w.at[:, pl.ds(0, HD)], in_sem.at[1])
    load_wv = pltpu.make_async_copy(wv_hbm, w.at[:, pl.ds(HD, HD)], in_sem.at[2])
    load_hs = pltpu.make_async_copy(hs_hbm.at[0], hs, in_sem.at[3])
    load_kc = pltpu.make_async_copy(kc_hbm.at[0], kk.at[pl.ds(0, CTX)], in_sem.at[4])
    load_vc = pltpu.make_async_copy(
        vc_hbm.at[0], vv.at[pl.ds(0, CTX), pl.ds(0, HD)], in_sem.at[5]
    )
    load_tk = pltpu.make_async_copy(tk_hbm, tk, in_sem.at[6])
    load_tv = pltpu.make_async_copy(tv_hbm, tv, in_sem.at[7])
    for copy in (load_hs, load_wk, load_wv, load_kc, load_vc, load_tk, load_tv):
        copy.start()

    barrier = pltpu.get_barrier_semaphore()
    for k in range(1, n_req):
        pl.semaphore_signal(
            barrier, inc=1, device_id={"req": lax.rem(me + k, n_req)}, device_id_type=MESH
        )
    for k in range(1, n_tp):
        pl.semaphore_signal(
            barrier, inc=1, device_id={"tp": lax.rem(mt + k, n_tp)}, device_id_type=MESH
        )

    crow = cont_ref[...]
    pcol = jnp.sum(
        jnp.where(iota((CD, crow.shape[1]), 1) == me * CD + iota((CD, crow.shape[1]), 0), crow, 0),
        axis=1,
        keepdims=True,
    )
    eye = iota((CD, HD), 0) == iota((CD, HD), 1)
    prow = jnp.sum(jnp.where(eye, pcol, 0), axis=0, keepdims=True)
    earlier = (prow == pcol) & (iota((CD, HD), 1) < iota((CD, HD), 0))
    slot = jnp.sum(jnp.where(earlier, 1, 0), axis=1, keepdims=True)
    base = pcol * 32 + slot * 16
    KR = CD * 16
    trow = jnp.sum(
        jnp.where(iota((CD, KR), 0) == iota((CD, KR), 1) // 16, base, 0), axis=0, keepdims=True
    ) + lax.rem(iota((1, KR), 1), 16)
    brow = jnp.sum(jnp.where(eye, base, 0), axis=0, keepdims=True)
    own = iota((KR, HD), 1) == iota((KR, HD), 0) // 16
    tcol = jnp.sum(jnp.where(own, brow, 0), axis=1, keepdims=True) + lax.rem(
        iota((KR, 1), 0), 16
    )

    n_p = plen_ref.shape[1]
    plen = plen_ref[...]
    tlen = tlen_ref[...]
    clen = jnp.sum(
        jnp.where(iota((CD, n_p), 1) == pcol, plen, 0), axis=1, keepdims=True
    ) + jnp.sum(jnp.where(iota((CD, CD), 0) == iota((CD, CD), 1), tlen, 0), axis=1, keepdims=True)
    lrow = jnp.sum(jnp.where(eye, clen, 0), axis=0, keepdims=True)
    pos_new = jnp.sum(
        jnp.where(iota((ROWS, HD), 1) == iota((ROWS, HD), 0) // T, lrow, 0), axis=1, keepdims=True
    ) + lax.rem(iota((ROWS, 1), 0), T)
    freq = freq_ref[...]
    sign = jnp.where(iota((1, HD), 1) < HD // 2, -1.0, 1.0)
    angle = pos_new.astype(F32) * freq
    cos_new = jnp.cos(angle)
    sin_new = jnp.sin(angle) * sign

    def norm_block(load, store):
        total = None
        for j in range(0, D, 512):
            x = load(j).astype(F32)
            x = x * x
            for i in range(0, 512, HD):
                total = x[:, i : i + HD] if total is None else total + x[:, i : i + HD]
        factor = lax.rsqrt(jnp.sum(total, axis=1, keepdims=True) * (1.0 / D) + 1e-05)
        for j in range(0, D, 512):
            x = load(j).astype(F32)
            store(j, x * factor * gain_ref[:, j : j + 512])

    load_nh.wait()
    for r in range(0, ROWS, 16):

        def load_new(j, r=r):
            return nh[r : r + 16, j : j + 512]

        def store_new(j, x, r=r):
            sn[RP + r : RP + r + 16, j : j + 512] = x.astype(BF16)

        norm_block(load_new, store_new)

    NB = posb.shape[0]
    pos_row[...] = jnp.full(pos_row.shape, -1, I32)
    pos_row[:, 0:RECOMP] = rpos_ref[...]
    for j in range(0, NB, HD):
        chunk = pos_row[:, j : j + HD].astype(F32)
        posb[j : j + HD, :] = jnp.transpose(jnp.broadcast_to(chunk, (HD, HD)))

    def tables(i, carry):
        at = pl.ds(pl.multiple_of(i * 16, 16), 16)
        turned = posb[at, :] * freq
        ropec[at, :] = jnp.cos(turned)
        ropes[at, :] = jnp.sin(turned) * sign
        return carry

    lax.fori_loop(0, RP // 16, tables, 0)
    my_len = jnp.sum(jnp.where(iota((1, n_p), 1) == me, plen, 0), axis=1, keepdims=True).astype(F32)
    for b in range(0, CTX, HD):
        first = b // 10 // 8 * 8
        rows = min(24, NB - first)
        here = (b + iota((1, HD), 1)).astype(F32)
        same = jnp.where(posb[first : first + rows, :] == here, 1.0, 0.0)
        replaced = jnp.max(same, axis=0, keepdims=True)
        bias[:, b : b + HD] = jnp.where((replaced > 0.0) | (here >= my_len), NEG, 0.0)
    for b in range(0, KT - CTX, HD):
        if b < NB:
            at = pos_row[:, b : b + HD].astype(F32)
            bias[:, CTX + b : CTX + b + HD] = jnp.where((at < 0.0) | (at >= my_len), NEG, 0.0)
        else:
            bias[:, CTX + b : CTX + b + HD] = jnp.full((1, HD), NEG, F32)
    vv[:, HD:] = jnp.ones((KT, HD), BF16)
    kk[CTX:, :] = jnp.zeros((KT - CTX, HD), BF16)
    vv[CTX:, 0:HD] = jnp.zeros((KT - CTX, HD), BF16)

    qacc[...] = jnp.zeros_like(qacc)

    def query_chunk(i, carry):
        pltpu.make_async_copy(wq_hbm.at[pl.ds(0, CH)], wq.at[i], wq_sem.at[i]).wait()
        x = sn[RP : RP + ROWS, pl.ds(pl.multiple_of(i * CH, CH), CH)]
        qacc[...] += dot(x, wq[i])
        return carry

    lax.fori_loop(0, n_ch, query_chunk, 0)
    for g in range(G):
        x = qacc[:, g * HD : (g + 1) * HD]
        x = x * cos_new + pltpu.roll(x, HD // 2, 1) * sin_new
        qs[g * ROWS : (g + 1) * ROWS, :] = x.astype(BF16)
    krow = iota((KR, G * ROWS), 0)
    picks = (lax.rem(krow, 16) // T) * ROWS + (krow // 16) * T + lax.rem(krow, T)
    qt[...] = dot(onehot(iota((KR, G * ROWS), 1) == picks), qs[...]).astype(BF16)
    n_x = n_req * 32
    sent = dot(onehot(iota((n_x, KR), 0) == trow), qt[...]).astype(BF16)
    for p in range(n_req):
        xs[p] = sent[p * 32 : (p + 1) * 32]

    pl.semaphore_wait(barrier, n_req + n_tp - 2)

    def peer(k):
        z = lax.rem(me // inner + k // inner, outer)
        y = lax.rem(lax.rem(me, inner) + lax.rem(k, inner), inner)
        return z * inner + y

    def query_copy(slot_at, to_dev):
        return pltpu.make_async_remote_copy(
            src_ref=xs.at[slot_at],
            dst_ref=rq.at[me],
            send_sem=qsend.at[slot_at],
            recv_sem=qrecv.at[me],
            device_id={"req": to_dev},
            device_id_type=MESH,
        )

    def query_arrival(src):
        return pltpu.make_async_remote_copy(
            src_ref=xs.at[src],
            dst_ref=rq.at[src],
            send_sem=qsend.at[src],
            recv_sem=qrecv.at[src],
            device_id={"req": src},
            device_id_type=MESH,
        )

    for k in range(1, n_req):
        to_dev = lax.rem(me + k, n_req)
        query_copy(to_dev, to_dev).start()
    rq[me] = xs[me]

    load_hs.wait()

    def stored_block(i, carry):
        at = pl.ds(pl.multiple_of(i * 16, 16), 16)

        def load_old(j):
            return hs[at, j : j + 512]

        def store_old(j, x):
            sn[at, j : j + 512] = x.astype(BF16)

        norm_block(load_old, store_old)
        return carry

    lax.fori_loop(0, RECOMP // 16, stored_block, 0)
    if RECOMP < RP:
        last = RECOMP // 16 * 16
        sn[last:RP, :] = jnp.zeros((RP - last, D), BF16)
        if last < RECOMP:

            def load_last(j):
                return hs[last:RECOMP, j : j + 512]

            def store_last(j, x):
                sn[last:RECOMP, j : j + 512] = x.astype(BF16)

            norm_block(load_last, store_last)
    load_wk.wait()
    load_wv.wait()
    kvacc[...] = jnp.zeros_like(kvacc)

    def kv_chunk(i, carry):
        at = pl.ds(pl.multiple_of(i * CH, CH), CH)
        kvacc[...] += dot(sn[:, at], w[at, :])
        return carry

    lax.fori_loop(0, D // CH, kv_chunk, 0)
    x = kvacc[0:RP, 0:HD]
    x = x * ropec[0:RP, :] + pltpu.roll(x, HD // 2, 1) * ropes[0:RP, :]
    load_kc.wait()
    load_vc.wait()
    kk[CTX : CTX + RP, :] = x.astype(BF16)
    vv[CTX : CTX + RP, 0:HD] = kvacc[0:RP, HD:].astype(BF16)
    x = kvacc[RP : RP + ROWS, 0:HD]
    key_new = (x * cos_new + pltpu.roll(x, HD // 2, 1) * sin_new).astype(BF16)
    value_new = kvacc[RP : RP + ROWS, HD:].astype(BF16)

    BC = 512
    NS = inner
    NR = NS * 32

    def prefix_block(i, carry):
        peers = [peer(n_req - 1 - i * NS - j) for j in range(NS)]
        for j in range(NS):

            @pl.when((i < n_req // NS - 1) | (j < NS - 1))
            def _(j=j):
                query_arrival(peers[j]).wait_recv()

        q = jnp.concatenate([rq[p] for p in peers], axis=0)
        top = None
        for j in range(0, KT, BC):
            s = dot_t(q, kk[j : j + BC, :]) + bias[:, j : j + BC]
            s_buf[:, j : j + BC] = s
            for b in range(0, BC, HD):
                part = s[:, b : b + HD]
                top = part if top is None else jnp.maximum(top, part)
        high = jnp.max(top, axis=1, keepdims=True) * scale
        acc = jnp.zeros((NR, 2 * HD), F32)
        for j in range(0, KT, BC):
            weights = jnp.exp2(s_buf[:, j : j + BC] * scale - high).astype(BF16)
            acc = acc + dot(weights, vv[j : j + BC, :])
        total = acc[:, HD:]
        out = acc[:, 0:HD] / total
        lse = jnp.transpose(high + jnp.log2(total))
        row = iota((32, HD), 0)
        for j in range(NS):
            stat = lse[0:32, :]
            if j:
                stat = pltpu.roll(stat, HD - 32 * j, 1)
            first = stat.astype(BF16).astype(F32)
            second = (stat - first).astype(BF16).astype(F32)
            third = stat - first - second
            block = jnp.where(
                row == 14,
                first,
                jnp.where(row == 15, second, jnp.where(row == 30, third, out[32 * j : 32 * j + 32])),
            )
            rs[peers[j]] = block.astype(BF16)
        for j in range(NS):

            @pl.when((i < n_req // NS - 1) | (j < NS - 1))
            def _(j=j):
                pltpu.make_async_remote_copy(
                    src_ref=rs.at[peers[j]],
                    dst_ref=rr.at[me],
                    send_sem=rsend.at[peers[j]],
                    recv_sem=rrecv.at[me],
                    device_id={"req": peers[j]},
                    device_id_type=MESH,
                ).start()

        return carry

    lax.fori_loop(0, n_req // NS, prefix_block, 0)
    rr[me] = rs[me]

    load_tk.wait()
    load_tv.wait()

    def tail_scores(c, carry):
        at = pl.ds(pl.multiple_of(c * 16, 16), 16)
        st[at, :] = dot_t(qt[at, :], tk[c])
        return carry

    lax.fori_loop(0, CD, tail_scores, 0)
    tlcol = jnp.sum(
        jnp.where(iota((KR, CD), 1) == iota((KR, CD), 0) // 16, tlen, 0), axis=1, keepdims=True
    )
    mask = iota((KR, TAIL), 1) < tlcol
    s = jnp.where(mask, st[...], NEG)
    m_t = jnp.max(s, axis=1, keepdims=True) * scale
    weights = jnp.where(mask, jnp.exp2(s * scale - m_t), 0.0).astype(BF16).astype(F32)
    l_t = jnp.sum(weights, axis=1, keepdims=True)
    st[...] = weights

    def tail_out(c, carry):
        at = pl.ds(pl.multiple_of(c * 16, 16), 16)
        to[at, :] = dot(st[at, :].astype(BF16), tv[c])
        return carry

    lax.fori_loop(0, CD, tail_out, 0)

    q32 = qt[...].astype(F32)
    hrow = iota((KR, ROWS), 0)
    odd = lax.rem(iota((KR, 1), 0), T) == 1
    pick0 = onehot(iota((KR, ROWS), 1) == (hrow // 16) * T)
    pick1 = onehot(iota((KR, ROWS), 1) == (hrow // 16) * T + 1)
    s0 = jnp.sum(q32 * dot(pick0, key_new), axis=1, keepdims=True) * scale
    s1 = jnp.where(odd, jnp.sum(q32 * dot(pick1, key_new), axis=1, keepdims=True) * scale, NEG)
    m_f = jnp.maximum(s0, s1)
    w0 = jnp.exp2(s0 - m_f).astype(BF16).astype(F32)
    w1 = jnp.where(odd, jnp.exp2(s1 - m_f), 0.0).astype(BF16).astype(F32)
    l_f = w0 + w1
    o_f = w0 * dot(pick0, value_new) + w1 * dot(pick1, value_new)

    for k in range(1, n_req):
        src = lax.rem(me + k, n_req)
        pltpu.make_async_remote_copy(
            src_ref=rs.at[src],
            dst_ref=rr.at[src],
            send_sem=rsend.at[src],
            recv_sem=rrecv.at[src],
            device_id={"req": src},
            device_id_type=MESH,
        ).wait_recv()
    parts = jnp.concatenate([rr[p] for p in range(n_req)], axis=0)
    lane = iota((KR, n_x), 1)
    o_p = dot(onehot(lane == tcol), parts)
    inside = lax.rem(lane, 32)
    stat_at = ((inside == 14) | (inside == 15) | (inside == 30)) & (lane // 32 == tcol // 32)
    stats = dot(onehot(stat_at), parts)
    lse_p = jnp.sum(
        jnp.where(iota((KR, HD), 1) == lax.rem(tcol, 32), stats, 0.0), axis=1, keepdims=True
    )

    top = jnp.maximum(jnp.maximum(lse_p, m_t), m_f)
    f_p = jnp.exp2(lse_p - top)
    f_t = jnp.exp2(m_t - top)
    f_f = jnp.exp2(m_f - top)
    numer = f_p * o_p + f_t * to[...] + f_f * o_f
    denom = f_p + f_t * l_t + f_f * l_f
    attended = (numer / denom).astype(BF16)
    brow2 = iota((G * ROWS, KR), 0)
    back = (lax.rem(brow2, ROWS) // T) * 16 + (brow2 // ROWS) * T + lax.rem(brow2, T)
    final = dot(onehot(iota((G * ROWS, KR), 1) == back), attended)
    partial = jnp.zeros((ROWS, HD), F32)
    for g in range(G):
        x = final[g * ROWS : (g + 1) * ROWS]
        out_ref[:, g * HD : (g + 1) * HD] = x.astype(BF16)
        partial = partial + x * sw_ref[:, g * HD : (g + 1) * HD]
    column = jnp.sum(partial, axis=1, keepdims=True)
    line = jnp.sum(
        jnp.where(iota((ROWS, HD), 0) == iota((ROWS, HD), 1) * T + 1, column, 0.0),
        axis=0,
        keepdims=True,
    )
    line = jnp.broadcast_to(line, (8, HD))
    scs[...] = line
    scr[mt] = line

    def score_copy(slot_at, k, dev):
        return pltpu.make_async_remote_copy(
            src_ref=scs,
            dst_ref=scr.at[slot_at],
            send_sem=ssend.at[k],
            recv_sem=srecv.at[slot_at],
            device_id={"tp": dev},
            device_id_type=MESH,
        )

    for k in range(1, n_tp):
        score_copy(mt, k, lax.rem(mt + k, n_tp)).start()
    for k in range(1, n_tp):
        src = lax.rem(mt + k, n_tp)
        score_copy(src, k, src).wait_recv()
    total = scr[0]
    for k in range(1, n_tp):
        total = total + scr[k]
    score_ref[...] = total

    for k in range(1, n_tp):
        dev = lax.rem(mt + k, n_tp)
        score_copy(dev, k, dev).wait_send()
    for k in range(1, n_req):
        dev = lax.rem(me + k, n_req)
        query_copy(dev, dev).wait_send()
        pltpu.make_async_remote_copy(
            src_ref=rs.at[dev],
            dst_ref=rr.at[me],
            send_sem=rsend.at[dev],
            recv_sem=rrecv.at[me],
            device_id={"req": dev},
            device_id_type=MESH,
        ).wait_send()


def per_device(
    inner,
    n_req,
    n_tp,
    new_hidden,
    norm_gain,
    w_query,
    w_key,
    w_value,
    hidden_store,
    key_cache,
    value_cache,
    tail_keys,
    tail_values,
    prompt_len,
    tail_len,
    recomp_pos,
    cont_prompt,
    score_weight,
):
    CD, T, D = new_hidden.shape
    QW = w_query.shape[1]
    G = QW // HD
    CTX = key_cache.shape[1]
    TAIL = tail_keys.shape[1]
    RECOMP = hidden_store.shape[1]
    ROWS = CD * T
    RP = -(-RECOMP // 32) * 32
    NB = -(-RECOMP // HD) * HD
    KT = CTX + 512
    CH = 512
    KR = CD * 16
    NR = inner * 32
    half = HD // 2
    freq = THETA ** (-2.0 * np.arange(half, dtype=np.float64) / HD)
    freq = np.concatenate([freq, freq]).astype(np.float32)[None, :]
    dims = (n_req, n_tp, inner, D, CTX, TAIL, RECOMP, CD, G)
    hbm = pl.BlockSpec(memory_space=pl.ANY)
    vmem = pl.BlockSpec(memory_space=pltpu.VMEM)
    dma = pltpu.SemaphoreType.DMA
    attended, scores = pl.pallas_call(
        functools.partial(kernel, dims),
        out_shape=(
            jax.ShapeDtypeStruct((ROWS, QW), BF16),
            jax.ShapeDtypeStruct((8, HD), F32),
        ),
        in_specs=[hbm, vmem] + [hbm] * 8 + [vmem] * 6,
        out_specs=(vmem, vmem),
        scratch_shapes=[
            pltpu.VMEM((ROWS, D), BF16),
            pltpu.VMEM((D // CH, CH, QW), BF16),
            pltpu.VMEM((D, 2 * HD), BF16),
            pltpu.VMEM((RECOMP, D), BF16),
            pltpu.VMEM((RP + ROWS, D), BF16),
            pltpu.VMEM((KT, HD), BF16),
            pltpu.VMEM((KT, 2 * HD), BF16),
            pltpu.VMEM((CD, TAIL, HD), BF16),
            pltpu.VMEM((CD, TAIL, HD), BF16),
            pltpu.VMEM((1, NB), I32),
            pltpu.VMEM((NB, HD), F32),
            pltpu.VMEM((RP, HD), F32),
            pltpu.VMEM((RP, HD), F32),
            pltpu.VMEM((1, KT), F32),
            pltpu.VMEM((ROWS, QW), F32),
            pltpu.VMEM((RP + ROWS, 2 * HD), F32),
            pltpu.VMEM((G * ROWS, HD), BF16),
            pltpu.VMEM((KR, HD), BF16),
            pltpu.VMEM((n_req, 32, HD), BF16),
            pltpu.VMEM((n_req, 32, HD), BF16),
            pltpu.VMEM((NR, KT), F32),
            pltpu.VMEM((n_req, 32, HD), BF16),
            pltpu.VMEM((n_req, 32, HD), BF16),
            pltpu.VMEM((KR, TAIL), F32),
            pltpu.VMEM((KR, HD), F32),
            pltpu.VMEM((8, HD), F32),
            pltpu.VMEM((n_tp, 8, HD), F32),
            dma((8,)),
            dma((D // CH,)),
            dma((n_req,)),
            dma((n_req,)),
            dma((n_req,)),
            dma((n_req,)),
            dma((n_tp,)),
            dma((n_tp,)),
        ],
        compiler_params=pltpu.CompilerParams(
            collective_id=0, has_side_effects=True, vmem_limit_bytes=56 * 1024 * 1024
        ),
        name="decode",
    )(
        new_hidden.reshape(ROWS, D),
        norm_gain.reshape(1, D),
        w_query,
        w_key,
        w_value,
        hidden_store,
        key_cache,
        value_cache,
        tail_keys,
        tail_values,
        prompt_len.reshape(1, -1),
        tail_len.reshape(1, -1),
        recomp_pos,
        cont_prompt.reshape(1, -1),
        score_weight.reshape(1, -1),
        jnp.asarray(freq),
    )
    return attended.reshape(CD, T, QW), scores[0, :CD]


def solution(mesh):
    placed = (
        P("req", None, None),
        P(),
        P(None, "tp"),
        P(None, "tp"),
        P(None, "tp"),
        P("req", None, None),
        P("req", None, "tp"),
        P("req", None, "tp"),
        P("req", None, "tp"),
        P("req", None, "tp"),
        P(),
        P("req"),
        P("req", None),
        P(),
        P("tp"),
    )
    n_req = mesh.shape["req"]
    inner = 4 if n_req % 4 == 0 else 1
    return jax.shard_map(
        functools.partial(per_device, inner, n_req, mesh.shape["tp"]),
        mesh=mesh,
        in_specs=placed,
        out_specs=(P("req", None, "tp"), P("req")),
        check_vma=False,
    )
```

```python
import functools
import math

import jax
import jax.numpy as jnp
import numpy as np
from jax import lax
from jax.experimental import pallas as pl
from jax.experimental.pallas import tpu as pltpu
from jax.sharding import PartitionSpec as P

MESH = pl.DeviceIdType.MESH
HD = 128
NEG = -1e30
THETA = 5000000.0
LOG2E = math.log2(math.e)
F32 = jnp.float32
BF16 = jnp.bfloat16
I32 = jnp.int32


def iota(shape, dim):
    return lax.broadcasted_iota(I32, shape, dim)


def dot(a, b):
    return jnp.dot(a, b, preferred_element_type=F32)


def dot_t(a, b):
    return lax.dot_general(a, b, (((1,), (1,)), ((), ())), preferred_element_type=F32)


def onehot(mask):
    return jnp.where(mask, 1.0, 0.0).astype(BF16)


def kernel(
    dims,
    nh_hbm,
    gain_hbm,
    wq_hbm,
    wk_hbm,
    wv_hbm,
    hs_hbm,
    kc_hbm,
    vc_hbm,
    tk_hbm,
    tv_hbm,
    plen_hbm,
    tlen_hbm,
    rpos_hbm,
    cont_hbm,
    sw_hbm,
    freq_hbm,
    out_ref,
    score_ref,
    nh,
    gain_ref,
    plen_ref,
    tlen_ref,
    rpos_ref,
    cont_ref,
    sw_ref,
    freq_ref,
    wq,
    w,
    hs,
    sn,
    kk,
    vv,
    tk,
    tv,
    pos_row,
    posb,
    ropec,
    ropes,
    bias,
    qacc,
    kvacc,
    qs,
    qt,
    xs,
    rq,
    s_buf,
    rs,
    rr,
    st,
    to,
    scs,
    scr,
    in_sem,
    nh_sem,
    wq_sem,
    qsend,
    qrecv,
    rsend,
    rrecv,
    ssend,
    srecv,
):
    n_req, n_tp, inner, D, CTX, TAIL, RECOMP, CD, G = dims
    T = 2
    ROWS = CD * T
    RP = -(-RECOMP // 32) * 32
    KT = kk.shape[0]
    outer = n_req // inner
    me = lax.axis_index("req")
    mt = lax.axis_index("tp")
    scale = HD ** (-0.5) * LOG2E
    CH = wq.shape[1]
    n_ch = wq.shape[0]

    loads_nh = [
        pltpu.make_async_copy(nh_hbm.at[c], nh.at[pl.ds(c * T, T)], nh_sem.at[c]) for c in range(CD)
    ]
    for copy in loads_nh:
        copy.start()
    small = (
        (gain_hbm, gain_ref),
        (plen_hbm, plen_ref),
        (tlen_hbm, tlen_ref),
        (rpos_hbm, rpos_ref),
        (cont_hbm, cont_ref),
        (sw_hbm, sw_ref),
        (freq_hbm, freq_ref),
    )
    loads_small = [
        pltpu.make_async_copy(src, dst, in_sem.at[8 + i]) for i, (src, dst) in enumerate(small)
    ]
    for copy in loads_small:
        copy.start()
    loads_q = [
        pltpu.make_async_copy(wq_hbm.at[pl.ds(i * CH, CH)], wq.at[i], wq_sem.at[i])
        for i in range(n_ch)
    ]
    DEPTH = min(6, n_ch)
    for copy in loads_q[:DEPTH]:
        copy.start()
    load_wk = pltpu.make_async_copy(wk_hbm, w.at[:, pl.ds(0, HD)], in_sem.at[1])
    load_wv = pltpu.make_async_copy(wv_hbm, w.at[:, pl.ds(HD, HD)], in_sem.at[2])
    load_hs = pltpu.make_async_copy(hs_hbm.at[0], hs, in_sem.at[3])
    load_kc = pltpu.make_async_copy(kc_hbm.at[0], kk.at[pl.ds(0, CTX)], in_sem.at[4])
    load_vc = pltpu.make_async_copy(
        vc_hbm.at[0], vv.at[pl.ds(0, CTX), pl.ds(0, HD)], in_sem.at[5]
    )
    load_tk = pltpu.make_async_copy(tk_hbm, tk, in_sem.at[6])
    load_tv = pltpu.make_async_copy(tv_hbm, tv, in_sem.at[7])
    after = loads_q[DEPTH:] + [load_hs, load_wk, load_wv, load_kc, load_vc, load_tk, load_tv]

    barrier = pltpu.get_barrier_semaphore()
    for k in range(1, n_req):
        pl.semaphore_signal(
            barrier, inc=1, device_id={"req": lax.rem(me + k, n_req)}, device_id_type=MESH
        )
    for k in range(1, n_tp):
        pl.semaphore_signal(
            barrier, inc=1, device_id={"tp": lax.rem(mt + k, n_tp)}, device_id_type=MESH
        )

    vv[:, HD:] = jnp.ones((KT, HD), BF16)
    kk[CTX:, :] = jnp.zeros((KT - CTX, HD), BF16)
    vv[CTX:, 0:HD] = jnp.zeros((KT - CTX, HD), BF16)

    for copy in loads_small:
        copy.wait()

    crow = cont_ref[...]
    pcol = jnp.sum(
        jnp.where(iota((CD, crow.shape[1]), 1) == me * CD + iota((CD, crow.shape[1]), 0), crow, 0),
        axis=1,
        keepdims=True,
    )
    eye = iota((CD, HD), 0) == iota((CD, HD), 1)
    prow = jnp.sum(jnp.where(eye, pcol, 0), axis=0, keepdims=True)
    earlier = (prow == pcol) & (iota((CD, HD), 1) < iota((CD, HD), 0))
    slot = jnp.sum(jnp.where(earlier, 1, 0), axis=1, keepdims=True)
    base = pcol * 32 + slot * 16
    KR = CD * 16
    QR = G * ROWS
    qcol = iota((1, QR), 1)
    trow = jnp.sum(
        jnp.where(iota((CD, QR), 0) == lax.rem(iota((CD, QR), 1), ROWS) // T, base, 0),
        axis=0,
        keepdims=True,
    ) + (qcol // ROWS * T + lax.rem(qcol, T))
    brow = jnp.sum(jnp.where(eye, base, 0), axis=0, keepdims=True)
    own = iota((KR, HD), 1) == iota((KR, HD), 0) // 16
    tcol = jnp.sum(jnp.where(own, brow, 0), axis=1, keepdims=True) + lax.rem(
        iota((KR, 1), 0), 16
    )

    n_p = plen_ref.shape[1]
    plen = plen_ref[...]
    tlen = tlen_ref[...]
    clen = jnp.sum(
        jnp.where(iota((CD, n_p), 1) == pcol, plen, 0), axis=1, keepdims=True
    ) + jnp.sum(jnp.where(iota((CD, CD), 0) == iota((CD, CD), 1), tlen, 0), axis=1, keepdims=True)
    lrow = jnp.sum(jnp.where(eye, clen, 0), axis=0, keepdims=True)
    pos_new = jnp.sum(
        jnp.where(iota((ROWS, HD), 1) == iota((ROWS, HD), 0) // T, lrow, 0), axis=1, keepdims=True
    ) + lax.rem(iota((ROWS, 1), 0), T)
    freq = freq_ref[...]
    sign = jnp.where(iota((1, HD), 1) < HD // 2, -1.0, 1.0)
    angle = pos_new.astype(F32) * freq
    cos_new = jnp.cos(angle)
    sin_new = jnp.sin(angle) * sign

    def norm_block(load, store):
        total = None
        for j in range(0, D, 512):
            x = load(j).astype(F32)
            x = x * x
            for i in range(0, 512, HD):
                total = x[:, i : i + HD] if total is None else total + x[:, i : i + HD]
        factor = lax.rsqrt(jnp.sum(total, axis=1, keepdims=True) * (1.0 / D) + 1e-05)
        for j in range(0, D, 512):
            x = load(j).astype(F32)
            store(j, x * factor * gain_ref[:, j : j + 512])

    for copy in loads_nh:
        copy.wait()
    for r in range(0, ROWS, ROWS):

        def load_new(j, r=r):
            return nh[r : r + ROWS, j : j + 512]

        def store_new(j, x, r=r):
            sn[RP + r : RP + r + ROWS, j : j + 512] = x.astype(BF16)

        norm_block(load_new, store_new)

    for i in range(n_ch):
        loads_q[i].wait()
        for copy in after[i : i + 1] if i < n_ch - 1 else after[i:]:
            copy.start()
        part = dot(sn[RP : RP + ROWS, i * CH : (i + 1) * CH], wq[i])
        if i == 0:
            qacc[...] = part
        else:
            qacc[...] += part
    for g in range(G):
        x = qacc[:, g * HD : (g + 1) * HD]
        x = x * cos_new + pltpu.roll(x, HD // 2, 1) * sin_new
        qs[g * ROWS : (g + 1) * ROWS, :] = x.astype(BF16)
    n_x = n_req * 32
    sent = dot(onehot(iota((n_x, QR), 0) == trow), qs[...]).astype(BF16)
    for p in range(n_req):
        xs[p] = sent[p * 32 : (p + 1) * 32]

    pl.semaphore_wait(barrier, n_req + n_tp - 2)

    def peer(k):
        z = lax.rem(me // inner + k // inner, outer)
        y = lax.rem(lax.rem(me, inner) + lax.rem(k, inner), inner)
        return z * inner + y

    def query_copy(slot_at, to_dev):
        return pltpu.make_async_remote_copy(
            src_ref=xs.at[slot_at],
            dst_ref=rq.at[me],
            send_sem=qsend.at[slot_at],
            recv_sem=qrecv.at[me],
            device_id={"req": to_dev},
            device_id_type=MESH,
        )

    def query_arrival(src):
        return pltpu.make_async_remote_copy(
            src_ref=xs.at[src],
            dst_ref=rq.at[src],
            send_sem=qsend.at[src],
            recv_sem=qrecv.at[src],
            device_id={"req": src},
            device_id_type=MESH,
        )

    for k in range(1, n_req):
        to_dev = lax.rem(me + k, n_req)
        query_copy(to_dev, to_dev).start()
    rq[me] = xs[me]
    krow = iota((KR, G * ROWS), 0)
    picks = (lax.rem(krow, 16) // T) * ROWS + (krow // 16) * T + lax.rem(krow, T)
    qt[...] = dot(onehot(iota((KR, G * ROWS), 1) == picks), qs[...]).astype(BF16)

    NB = posb.shape[0]
    pos_row[...] = jnp.full(pos_row.shape, -1, I32)
    pos_row[:, 0:RECOMP] = rpos_ref[...]
    for j in range(0, NB, HD):
        chunk = pos_row[:, j : j + HD].astype(F32)
        posb[j : j + HD, :] = jnp.transpose(jnp.broadcast_to(chunk, (HD, HD)))

    def tables(i, carry):
        at = pl.ds(pl.multiple_of(i * 16, 16), 16)
        turned = posb[at, :] * freq
        ropec[at, :] = jnp.cos(turned)
        ropes[at, :] = jnp.sin(turned) * sign
        return carry

    lax.fori_loop(0, RP // 16, tables, 0)
    my_len = jnp.sum(jnp.where(iota((1, n_p), 1) == me, plen, 0), axis=1, keepdims=True).astype(F32)
    for b in range(0, CTX, HD):
        first = b // 10 // 8 * 8
        rows = min(24, NB - first)
        here = (b + iota((1, HD), 1)).astype(F32)
        same = jnp.where(posb[first : first + rows, :] == here, 1.0, 0.0)
        replaced = jnp.max(same, axis=0, keepdims=True)
        bias[:, b : b + HD] = jnp.where((replaced > 0.0) | (here >= my_len), NEG, 0.0)
    for b in range(0, KT - CTX, HD):
        if b < NB:
            at = pos_row[:, b : b + HD].astype(F32)
            bias[:, CTX + b : CTX + b + HD] = jnp.where((at < 0.0) | (at >= my_len), NEG, 0.0)
        else:
            bias[:, CTX + b : CTX + b + HD] = jnp.full((1, HD), NEG, F32)

    load_hs.wait()

    NB_ROWS = 80 if RECOMP >= 80 else 16

    def stored_block(i, carry):
        at = pl.ds(pl.multiple_of(i * NB_ROWS, 16), NB_ROWS)

        def load_old(j):
            return hs[at, j : j + 512]

        def store_old(j, x):
            sn[at, j : j + 512] = x.astype(BF16)

        norm_block(load_old, store_old)
        return carry

    lax.fori_loop(0, RECOMP // NB_ROWS, stored_block, 0)
    if RECOMP < RP:
        last = RECOMP // NB_ROWS * NB_ROWS
        sn[last:RP, :] = jnp.zeros((RP - last, D), BF16)
        if last < RECOMP:

            def load_last(j):
                return hs[last:RECOMP, j : j + 512]

            def store_last(j, x):
                sn[last:RECOMP, j : j + 512] = x.astype(BF16)

            norm_block(load_last, store_last)
    load_wk.wait()
    load_wv.wait()
    KC = D // 4
    kvacc[...] = dot(sn[:, 0:KC], w[0:KC, :])

    def kv_chunk(i, carry):
        at = pl.ds(pl.multiple_of(i * KC, HD), KC)
        kvacc[...] += dot(sn[:, at], w[at, :])
        return carry

    lax.fori_loop(1, 4, kv_chunk, 0)
    x = kvacc[0:RP, 0:HD]
    x = x * ropec[0:RP, :] + pltpu.roll(x, HD // 2, 1) * ropes[0:RP, :]
    load_kc.wait()
    load_vc.wait()
    kk[CTX : CTX + RP, :] = x.astype(BF16)
    vv[CTX : CTX + RP, 0:HD] = kvacc[0:RP, HD:].astype(BF16)
    x = kvacc[RP : RP + ROWS, 0:HD]
    key_new = (x * cos_new + pltpu.roll(x, HD // 2, 1) * sin_new).astype(BF16)
    value_new = kvacc[RP : RP + ROWS, HD:].astype(BF16)

    BC = 512
    NS = 2 * inner
    NR = NS * 32

    def prefix_block(i, carry):
        peers = [peer(n_req - 1 - i * NS - j) for j in range(NS)]
        for j in range(NS):

            @pl.when((i < n_req // NS - 1) | (j < NS - 1))
            def _(j=j):
                query_arrival(peers[j]).wait_recv()

        q = jnp.concatenate([rq[p] for p in peers], axis=0)
        top = None
        for j in range(0, KT, BC):
            s = dot_t(q, kk[j : j + BC, :]) + bias[:, j : j + BC]
            s_buf[:, j : j + BC] = s
            for b in range(0, BC, HD):
                part = s[:, b : b + HD]
                top = part if top is None else jnp.maximum(top, part)
        high = jnp.max(top, axis=1, keepdims=True) * scale
        acc = jnp.zeros((NR, 2 * HD), F32)
        for j in range(0, KT, BC):
            weights = jnp.exp2(s_buf[:, j : j + BC] * scale - high).astype(BF16)
            acc = acc + dot(weights, vv[j : j + BC, :])
        total = acc[:, HD:]
        out = acc[:, 0:HD] / total
        lse = high + jnp.log2(total)
        lses = [jnp.transpose(lse[r : r + HD]) for r in range(0, NR, HD)]
        row = iota((32, HD), 0)
        for j in range(NS):
            stat = lses[32 * j // HD][0:32, :]
            if 32 * j % HD:
                stat = pltpu.roll(stat, HD - 32 * j % HD, 1)
            first = stat.astype(BF16).astype(F32)
            second = (stat - first).astype(BF16).astype(F32)
            third = stat - first - second
            block = jnp.where(
                row == 14,
                first,
                jnp.where(row == 15, second, jnp.where(row == 30, third, out[32 * j : 32 * j + 32])),
            )
            rs[peers[j]] = block.astype(BF16)
        for j in range(NS):

            @pl.when((i < n_req // NS - 1) | (j < NS - 1))
            def _(j=j):
                pltpu.make_async_remote_copy(
                    src_ref=rs.at[peers[j]],
                    dst_ref=rr.at[me],
                    send_sem=rsend.at[peers[j]],
                    recv_sem=rrecv.at[me],
                    device_id={"req": peers[j]},
                    device_id_type=MESH,
                ).start()

        return carry

    lax.fori_loop(0, n_req // NS, prefix_block, 0)
    rr[me] = rs[me]

    load_tk.wait()
    load_tv.wait()

    def tail_scores(c, carry):
        at = pl.ds(pl.multiple_of(c * 16, 16), 16)
        st[at, :] = dot_t(qt[at, :], tk[c])
        return carry

    lax.fori_loop(0, CD, tail_scores, 0, unroll=True)
    tlcol = jnp.sum(
        jnp.where(iota((KR, CD), 1) == iota((KR, CD), 0) // 16, tlen, 0), axis=1, keepdims=True
    )
    mask = iota((KR, TAIL), 1) < tlcol
    s = jnp.where(mask, st[...], NEG)
    m_t = jnp.max(s, axis=1, keepdims=True) * scale
    weights = jnp.where(mask, jnp.exp2(s * scale - m_t), 0.0).astype(BF16).astype(F32)
    l_t = jnp.sum(weights, axis=1, keepdims=True)
    st[...] = weights

    def tail_out(c, carry):
        at = pl.ds(pl.multiple_of(c * 16, 16), 16)
        to[at, :] = dot(st[at, :].astype(BF16), tv[c])
        return carry

    lax.fori_loop(0, CD, tail_out, 0, unroll=True)

    q32 = qt[...].astype(F32)
    hrow = iota((KR, ROWS), 0)
    odd = lax.rem(iota((KR, 1), 0), T) == 1
    pick0 = onehot(iota((KR, ROWS), 1) == (hrow // 16) * T)
    pick1 = onehot(iota((KR, ROWS), 1) == (hrow // 16) * T + 1)
    s0 = jnp.sum(q32 * dot(pick0, key_new), axis=1, keepdims=True) * scale
    s1 = jnp.where(odd, jnp.sum(q32 * dot(pick1, key_new), axis=1, keepdims=True) * scale, NEG)
    m_f = jnp.maximum(s0, s1)
    w0 = jnp.exp2(s0 - m_f).astype(BF16).astype(F32)
    w1 = jnp.where(odd, jnp.exp2(s1 - m_f), 0.0).astype(BF16).astype(F32)
    l_f = w0 + w1
    o_f = w0 * dot(pick0, value_new) + w1 * dot(pick1, value_new)

    for k in range(1, n_req):
        src = lax.rem(me + k, n_req)
        pltpu.make_async_remote_copy(
            src_ref=rs.at[src],
            dst_ref=rr.at[src],
            send_sem=rsend.at[src],
            recv_sem=rrecv.at[src],
            device_id={"req": src},
            device_id_type=MESH,
        ).wait_recv()
    parts = jnp.concatenate([rr[p] for p in range(n_req)], axis=0)
    lane = iota((KR, n_x), 1)
    o_p = dot(onehot(lane == tcol), parts)
    inside = lax.rem(lane, 32)
    stat_at = ((inside == 14) | (inside == 15) | (inside == 30)) & (lane // 32 == tcol // 32)
    stats = dot(onehot(stat_at), parts)
    lse_p = jnp.sum(
        jnp.where(iota((KR, HD), 1) == lax.rem(tcol, 32), stats, 0.0), axis=1, keepdims=True
    )

    top = jnp.maximum(jnp.maximum(lse_p, m_t), m_f)
    f_p = jnp.exp2(lse_p - top)
    f_t = jnp.exp2(m_t - top)
    f_f = jnp.exp2(m_f - top)
    numer = f_p * o_p + f_t * to[...] + f_f * o_f
    denom = f_p + f_t * l_t + f_f * l_f
    attended = (numer / denom).astype(BF16)
    brow2 = iota((G * ROWS, KR), 0)
    back = (lax.rem(brow2, ROWS) // T) * 16 + (brow2 // ROWS) * T + lax.rem(brow2, T)
    final = dot(onehot(iota((G * ROWS, KR), 1) == back), attended)
    partial = jnp.zeros((ROWS, HD), F32)
    for g in range(G):
        x = final[g * ROWS : (g + 1) * ROWS]
        out_ref[:, g * HD : (g + 1) * HD] = x.astype(BF16)
        partial = partial + x * sw_ref[pl.ds(g * HD, HD)].reshape(1, HD)
    column = jnp.sum(partial, axis=1, keepdims=True)
    line = jnp.sum(
        jnp.where(iota((ROWS, HD), 0) == iota((ROWS, HD), 1) * T + 1, column, 0.0),
        axis=0,
        keepdims=True,
    )
    line = jnp.broadcast_to(line, (8, HD))
    scs[...] = line
    scr[mt] = line

    def score_copy(slot_at, k, dev):
        return pltpu.make_async_remote_copy(
            src_ref=scs,
            dst_ref=scr.at[slot_at],
            send_sem=ssend.at[k],
            recv_sem=srecv.at[slot_at],
            device_id={"tp": dev},
            device_id_type=MESH,
        )

    for k in range(1, n_tp):
        score_copy(mt, k, lax.rem(mt + k, n_tp)).start()
    for k in range(1, n_tp):
        src = lax.rem(mt + k, n_tp)
        score_copy(src, k, src).wait_recv()
    total = scr[0]
    for k in range(1, n_tp):
        total = total + scr[k]
    score_ref[...] = total

    for k in range(1, n_tp):
        dev = lax.rem(mt + k, n_tp)
        score_copy(dev, k, dev).wait_send()
    for k in range(1, n_req):
        dev = lax.rem(me + k, n_req)
        query_copy(dev, dev).wait_send()
        pltpu.make_async_remote_copy(
            src_ref=rs.at[dev],
            dst_ref=rr.at[me],
            send_sem=rsend.at[dev],
            recv_sem=rrecv.at[me],
            device_id={"req": dev},
            device_id_type=MESH,
        ).wait_send()


def per_device(
    inner,
    n_req,
    n_tp,
    new_hidden,
    norm_gain,
    w_query,
    w_key,
    w_value,
    hidden_store,
    key_cache,
    value_cache,
    tail_keys,
    tail_values,
    prompt_len,
    tail_len,
    recomp_pos,
    cont_prompt,
    score_weight,
):
    CD, T, D = new_hidden.shape
    QW = w_query.shape[1]
    G = QW // HD
    CTX = key_cache.shape[1]
    TAIL = tail_keys.shape[1]
    RECOMP = hidden_store.shape[1]
    ROWS = CD * T
    RP = -(-RECOMP // 32) * 32
    NB = -(-RECOMP // HD) * HD
    KT = CTX + 512
    CH = 512
    KR = CD * 16
    NR = 2 * inner * 32
    half = HD // 2
    freq = THETA ** (-2.0 * np.arange(half, dtype=np.float64) / HD)
    freq = np.concatenate([freq, freq]).astype(np.float32)[None, :]
    dims = (n_req, n_tp, inner, D, CTX, TAIL, RECOMP, CD, G)
    hbm = pl.BlockSpec(memory_space=pl.ANY)
    vmem = pl.BlockSpec(memory_space=pltpu.VMEM)
    dma = pltpu.SemaphoreType.DMA
    attended, scores = pl.pallas_call(
        functools.partial(kernel, dims),
        out_shape=(
            jax.ShapeDtypeStruct((ROWS, QW), BF16),
            jax.ShapeDtypeStruct((8, HD), F32),
        ),
        in_specs=[hbm] * 16,
        out_specs=(vmem, vmem),
        scratch_shapes=[
            pltpu.VMEM((ROWS, D), BF16),
            pltpu.VMEM((1, D), F32),
            pltpu.VMEM((1, prompt_len.shape[0]), I32),
            pltpu.VMEM((1, CD), I32),
            pltpu.VMEM((1, RECOMP), I32),
            pltpu.VMEM((1, cont_prompt.shape[0]), I32),
            pltpu.VMEM((QW,), F32),
            pltpu.VMEM((1, HD), F32),
            pltpu.VMEM((D // CH, CH, QW), BF16),
            pltpu.VMEM((D, 2 * HD), BF16),
            pltpu.VMEM((RECOMP, D), BF16),
            pltpu.VMEM((RP + ROWS, D), BF16),
            pltpu.VMEM((KT, HD), BF16),
            pltpu.VMEM((KT, 2 * HD), BF16),
            pltpu.VMEM((CD, TAIL, HD), BF16),
            pltpu.VMEM((CD, TAIL, HD), BF16),
            pltpu.VMEM((1, NB), I32),
            pltpu.VMEM((NB, HD), F32),
            pltpu.VMEM((RP, HD), F32),
            pltpu.VMEM((RP, HD), F32),
            pltpu.VMEM((1, KT), F32),
            pltpu.VMEM((ROWS, QW), F32),
            pltpu.VMEM((RP + ROWS, 2 * HD), F32),
            pltpu.VMEM((G * ROWS, HD), BF16),
            pltpu.VMEM((KR, HD), BF16),
            pltpu.VMEM((n_req, 32, HD), BF16),
            pltpu.VMEM((n_req, 32, HD), BF16),
            pltpu.VMEM((NR, KT), F32),
            pltpu.VMEM((n_req, 32, HD), BF16),
            pltpu.VMEM((n_req, 32, HD), BF16),
            pltpu.VMEM((KR, TAIL), F32),
            pltpu.VMEM((KR, HD), F32),
            pltpu.VMEM((8, HD), F32),
            pltpu.VMEM((n_tp, 8, HD), F32),
            dma((15,)),
            dma((CD,)),
            dma((D // CH,)),
            dma((n_req,)),
            dma((n_req,)),
            dma((n_req,)),
            dma((n_req,)),
            dma((n_tp,)),
            dma((n_tp,)),
        ],
        compiler_params=pltpu.CompilerParams(
            collective_id=0, has_side_effects=True, vmem_limit_bytes=67_043_328
        ),
        name="decode",
    )(
        new_hidden,
        norm_gain.reshape(1, D),
        w_query,
        w_key,
        w_value,
        hidden_store,
        key_cache,
        value_cache,
        tail_keys,
        tail_values,
        prompt_len.reshape(1, -1),
        tail_len.reshape(1, -1),
        recomp_pos,
        cont_prompt.reshape(1, -1),
        score_weight,
        jnp.asarray(freq),
    )
    return attended.reshape(CD, T, QW), scores[0, :CD]


def solution(mesh):
    placed = (
        P("req", None, None),
        P(),
        P(None, "tp"),
        P(None, "tp"),
        P(None, "tp"),
        P("req", None, None),
        P("req", None, "tp"),
        P("req", None, "tp"),
        P("req", None, "tp"),
        P("req", None, "tp"),
        P(),
        P("req"),
        P("req", None),
        P(),
        P("tp"),
    )
    n_req = mesh.shape["req"]
    inner = 4 if n_req % 4 == 0 else 1
    return jax.shard_map(
        functools.partial(per_device, inner, n_req, mesh.shape["tp"]),
        mesh=mesh,
        in_specs=placed,
        out_specs=(P("req", None, "tp"), P("req")),
        check_vma=False,
    )
```

```python
import functools
import math

import jax
import jax.numpy as jnp
import numpy as np
from jax import lax
from jax.experimental import pallas as pl
from jax.experimental.pallas import tpu as pltpu
from jax.sharding import PartitionSpec as P

MESH = pl.DeviceIdType.MESH
HD = 128
NEG = -1e30
THETA = 5000000.0
LOG2E = math.log2(math.e)
F32 = jnp.float32
BF16 = jnp.bfloat16
I32 = jnp.int32


def iota(shape, dim):
    return lax.broadcasted_iota(I32, shape, dim)


def dot(a, b):
    return jnp.dot(a, b, preferred_element_type=F32)


def dot_t(a, b):
    return lax.dot_general(a, b, (((1,), (1,)), ((), ())), preferred_element_type=F32)


def onehot(mask):
    return jnp.where(mask, 1.0, 0.0).astype(BF16)


def kernel(
    dims,
    nh_hbm,
    gain_hbm,
    wq_hbm,
    wk_hbm,
    wv_hbm,
    hs_hbm,
    kc_hbm,
    vc_hbm,
    tk_hbm,
    tv_hbm,
    plen_hbm,
    tlen_hbm,
    rpos_hbm,
    cont_hbm,
    sw_hbm,
    freq_hbm,
    out_ref,
    score_ref,
    nh,
    gain_ref,
    plen_ref,
    tlen_ref,
    rpos_ref,
    cont_ref,
    sw_ref,
    freq_ref,
    wq,
    w,
    hs,
    sn,
    kk,
    vv,
    tk,
    tv,
    pos_row,
    posb,
    ropec,
    ropes,
    bias,
    qacc,
    kvacc,
    qs,
    qt,
    xs,
    rq,
    s_buf,
    rs,
    rr,
    st,
    to,
    scs,
    scr,
    pick_o,
    pick_s,
    pick_b,
    outv,
    out_sem,
    in_sem,
    nh_sem,
    wq_sem,
    qsend,
    qrecv,
    rsend,
    rrecv,
    ssend,
    srecv,
):
    n_req, n_tp, inner, D, CTX, TAIL, RECOMP, CD, G = dims
    T = 2
    ROWS = CD * T
    RP = -(-RECOMP // 32) * 32
    KT = kk.shape[0]
    outer = n_req // inner
    me = lax.axis_index("req")
    mt = lax.axis_index("tp")
    scale = HD ** (-0.5) * LOG2E
    CH = wq.shape[1]
    n_ch = wq.shape[0]

    loads_nh = [
        pltpu.make_async_copy(nh_hbm.at[c], nh.at[pl.ds(c * T, T)], nh_sem.at[c]) for c in range(CD)
    ]
    for copy in loads_nh:
        copy.start()
    small = (
        (gain_hbm, gain_ref),
        (plen_hbm, plen_ref),
        (tlen_hbm, tlen_ref),
        (rpos_hbm, rpos_ref),
        (cont_hbm, cont_ref),
        (sw_hbm, sw_ref),
        (freq_hbm, freq_ref),
    )
    loads_small = [
        pltpu.make_async_copy(src, dst, in_sem.at[8 + i]) for i, (src, dst) in enumerate(small)
    ]
    for copy in loads_small:
        copy.start()
    loads_q = [
        pltpu.make_async_copy(wq_hbm.at[pl.ds(i * CH, CH)], wq.at[i], wq_sem.at[i])
        for i in range(n_ch)
    ]
    DEPTH = min(6, n_ch)
    for copy in loads_q[:DEPTH]:
        copy.start()
    load_wk = pltpu.make_async_copy(wk_hbm, w.at[:, pl.ds(0, HD)], in_sem.at[1])
    load_wv = pltpu.make_async_copy(wv_hbm, w.at[:, pl.ds(HD, HD)], in_sem.at[2])
    load_hs = pltpu.make_async_copy(hs_hbm.at[0], hs, in_sem.at[3])
    load_kc = pltpu.make_async_copy(kc_hbm.at[0], kk.at[pl.ds(0, CTX)], in_sem.at[4])
    load_vc = pltpu.make_async_copy(
        vc_hbm.at[0], vv.at[pl.ds(0, CTX), pl.ds(0, HD)], in_sem.at[5]
    )
    load_tk = pltpu.make_async_copy(tk_hbm, tk, in_sem.at[6])
    load_tv = pltpu.make_async_copy(tv_hbm, tv, in_sem.at[7])
    after = loads_q[DEPTH:] + [load_hs, load_wk, load_wv, load_kc, load_vc, load_tk, load_tv]

    barrier = pltpu.get_barrier_semaphore()
    for k in range(1, n_req):
        pl.semaphore_signal(
            barrier, inc=1, device_id={"req": lax.rem(me + k, n_req)}, device_id_type=MESH
        )
    for k in range(1, n_tp):
        pl.semaphore_signal(
            barrier, inc=1, device_id={"tp": lax.rem(mt + k, n_tp)}, device_id_type=MESH
        )

    vv[:, HD:] = jnp.ones((KT, HD), BF16)
    kk[CTX:, :] = jnp.zeros((KT - CTX, HD), BF16)
    vv[CTX:, 0:HD] = jnp.zeros((KT - CTX, HD), BF16)

    for copy in loads_small:
        copy.wait()

    crow = cont_ref[...]
    pcol = jnp.sum(
        jnp.where(iota((CD, crow.shape[1]), 1) == me * CD + iota((CD, crow.shape[1]), 0), crow, 0),
        axis=1,
        keepdims=True,
    )
    eye = iota((CD, HD), 0) == iota((CD, HD), 1)
    prow = jnp.sum(jnp.where(eye, pcol, 0), axis=0, keepdims=True)
    earlier = (prow == pcol) & (iota((CD, HD), 1) < iota((CD, HD), 0))
    slot = jnp.sum(jnp.where(earlier, 1, 0), axis=1, keepdims=True)
    base = pcol * 32 + slot * 16
    KR = CD * 16
    QR = G * ROWS
    qcol = iota((1, QR), 1)
    trow = jnp.sum(
        jnp.where(iota((CD, QR), 0) == lax.rem(iota((CD, QR), 1), ROWS) // T, base, 0),
        axis=0,
        keepdims=True,
    ) + (qcol // ROWS * T + lax.rem(qcol, T))
    brow = jnp.sum(jnp.where(eye, base, 0), axis=0, keepdims=True)
    own = iota((KR, HD), 1) == iota((KR, HD), 0) // 16
    tcol = jnp.sum(jnp.where(own, brow, 0), axis=1, keepdims=True) + lax.rem(
        iota((KR, 1), 0), 16
    )

    n_p = plen_ref.shape[1]
    plen = plen_ref[...]
    tlen = tlen_ref[...]
    clen = jnp.sum(
        jnp.where(iota((CD, n_p), 1) == pcol, plen, 0), axis=1, keepdims=True
    ) + jnp.sum(jnp.where(iota((CD, CD), 0) == iota((CD, CD), 1), tlen, 0), axis=1, keepdims=True)
    lrow = jnp.sum(jnp.where(eye, clen, 0), axis=0, keepdims=True)
    pos_new = jnp.sum(
        jnp.where(iota((ROWS, HD), 1) == iota((ROWS, HD), 0) // T, lrow, 0), axis=1, keepdims=True
    ) + lax.rem(iota((ROWS, 1), 0), T)
    freq = freq_ref[...]
    sign = jnp.where(iota((1, HD), 1) < HD // 2, -1.0, 1.0)
    angle = pos_new.astype(F32) * freq
    cos_new = jnp.cos(angle)
    sin_new = jnp.sin(angle) * sign

    def norm_block(load, store):
        total = None
        for j in range(0, D, 512):
            x = load(j).astype(F32)
            x = x * x
            for i in range(0, 512, HD):
                total = x[:, i : i + HD] if total is None else total + x[:, i : i + HD]
        factor = lax.rsqrt(jnp.sum(total, axis=1, keepdims=True) * (1.0 / D) + 1e-05)
        for j in range(0, D, 512):
            x = load(j).astype(F32)
            store(j, x * factor * gain_ref[:, j : j + 512])

    for copy in loads_nh:
        copy.wait()
    for r in range(0, ROWS, ROWS):

        def load_new(j, r=r):
            return nh[r : r + ROWS, j : j + 512]

        def store_new(j, x, r=r):
            sn[RP + r : RP + r + ROWS, j : j + 512] = x.astype(BF16)

        norm_block(load_new, store_new)

    for i in range(n_ch):
        loads_q[i].wait()
        for copy in after[i : i + 1] if i < n_ch - 1 else after[i:]:
            copy.start()
        part = dot(sn[RP : RP + ROWS, i * CH : (i + 1) * CH], wq[i])
        if i == 0:
            qacc[...] = part
        else:
            qacc[...] += part
    for g in range(G):
        x = qacc[:, g * HD : (g + 1) * HD]
        x = x * cos_new + pltpu.roll(x, HD // 2, 1) * sin_new
        qs[g * ROWS : (g + 1) * ROWS, :] = x.astype(BF16)
    n_x = n_req * 32
    sent = dot(onehot(iota((n_x, QR), 0) == trow), qs[...]).astype(BF16)
    for p in range(n_req):
        xs[p] = sent[p * 32 : (p + 1) * 32]

    pl.semaphore_wait(barrier, n_req + n_tp - 2)

    def peer(k):
        z = lax.rem(me // inner + k // inner, outer)
        y = lax.rem(lax.rem(me, inner) + lax.rem(k, inner), inner)
        return z * inner + y

    def query_copy(slot_at, to_dev):
        return pltpu.make_async_remote_copy(
            src_ref=xs.at[slot_at],
            dst_ref=rq.at[me],
            send_sem=qsend.at[slot_at],
            recv_sem=qrecv.at[me],
            device_id={"req": to_dev},
            device_id_type=MESH,
        )

    def query_arrival(src):
        return pltpu.make_async_remote_copy(
            src_ref=xs.at[src],
            dst_ref=rq.at[src],
            send_sem=qsend.at[src],
            recv_sem=qrecv.at[src],
            device_id={"req": src},
            device_id_type=MESH,
        )

    for k in range(1, n_req):
        to_dev = lax.rem(me + k, n_req)
        query_copy(to_dev, to_dev).start()
    rq[me] = xs[me]
    krow = iota((KR, G * ROWS), 0)
    picks = (lax.rem(krow, 16) // T) * ROWS + (krow // 16) * T + lax.rem(krow, T)
    qt[...] = dot(onehot(iota((KR, G * ROWS), 1) == picks), qs[...]).astype(BF16)

    NB = posb.shape[0]
    pos_row[...] = jnp.full(pos_row.shape, -1, I32)
    pos_row[:, 0:RECOMP] = rpos_ref[...]
    for j in range(0, NB, HD):
        chunk = pos_row[:, j : j + HD].astype(F32)
        posb[j : j + HD, :] = jnp.transpose(jnp.broadcast_to(chunk, (HD, HD)))

    def tables(i, carry):
        at = pl.ds(pl.multiple_of(i * 16, 16), 16)
        turned = posb[at, :] * freq
        ropec[at, :] = jnp.cos(turned)
        ropes[at, :] = jnp.sin(turned) * sign
        return carry

    lax.fori_loop(0, RP // 16, tables, 0)
    my_len = jnp.sum(jnp.where(iota((1, n_p), 1) == me, plen, 0), axis=1, keepdims=True).astype(F32)
    for b in range(0, CTX, HD):
        first = b // 10 // 8 * 8
        rows = min(24, NB - first)
        here = (b + iota((1, HD), 1)).astype(F32)
        same = jnp.where(posb[first : first + rows, :] == here, 1.0, 0.0)
        replaced = jnp.max(same, axis=0, keepdims=True)
        bias[:, b : b + HD] = jnp.where((replaced > 0.0) | (here >= my_len), NEG, 0.0)
    for b in range(0, KT - CTX, HD):
        if b < NB:
            at = pos_row[:, b : b + HD].astype(F32)
            bias[:, CTX + b : CTX + b + HD] = jnp.where((at < 0.0) | (at >= my_len), NEG, 0.0)
        else:
            bias[:, CTX + b : CTX + b + HD] = jnp.full((1, HD), NEG, F32)

    load_hs.wait()

    NB_ROWS = 80 if RECOMP >= 80 else 16

    def stored_block(i, carry):
        at = pl.ds(pl.multiple_of(i * NB_ROWS, 16), NB_ROWS)

        def load_old(j):
            return hs[at, j : j + 512]

        def store_old(j, x):
            sn[at, j : j + 512] = x.astype(BF16)

        norm_block(load_old, store_old)
        return carry

    lax.fori_loop(0, RECOMP // NB_ROWS, stored_block, 0)
    if RECOMP < RP:
        last = RECOMP // NB_ROWS * NB_ROWS
        sn[last:RP, :] = jnp.zeros((RP - last, D), BF16)
        if last < RECOMP:

            def load_last(j):
                return hs[last:RECOMP, j : j + 512]

            def store_last(j, x):
                sn[last:RECOMP, j : j + 512] = x.astype(BF16)

            norm_block(load_last, store_last)
    load_wk.wait()
    load_wv.wait()
    KC = D // 4
    kvacc[...] = dot(sn[:, 0:KC], w[0:KC, :])

    def kv_chunk(i, carry):
        at = pl.ds(pl.multiple_of(i * KC, HD), KC)
        kvacc[...] += dot(sn[:, at], w[at, :])
        return carry

    lax.fori_loop(1, 4, kv_chunk, 0)
    x = kvacc[0:RP, 0:HD]
    x = x * ropec[0:RP, :] + pltpu.roll(x, HD // 2, 1) * ropes[0:RP, :]
    load_kc.wait()
    load_vc.wait()
    kk[CTX : CTX + RP, :] = x.astype(BF16)
    vv[CTX : CTX + RP, 0:HD] = kvacc[0:RP, HD:].astype(BF16)
    x = kvacc[RP : RP + ROWS, 0:HD]
    key_new = (x * cos_new + pltpu.roll(x, HD // 2, 1) * sin_new).astype(BF16)
    value_new = kvacc[RP : RP + ROWS, HD:].astype(BF16)

    BC = 256
    RR = HD
    NS = 2 * inner
    NR = NS * 32

    def prefix_block(i):
        peers = [peer(n_req - 1 - i * NS - j) for j in range(NS)]
        for j in range(NS):

            if i < n_req // NS - 1 or j < NS - 1:
                query_arrival(peers[j]).wait_recv()

        q = jnp.concatenate([rq[p] for p in peers], axis=0)
        top = None
        for j in range(0, KT, BC):
            s = dot_t(q, kk[j : j + BC, :]) + bias[:, j : j + BC]
            s_buf[i, :, j : j + BC] = s
            for b in range(0, BC, HD):
                part = s[:, b : b + HD]
                top = part if top is None else jnp.maximum(top, part)
        high = jnp.max(top, axis=1, keepdims=True) * scale
        accs = []
        for r in range(0, NR, RR):
            acc = jnp.zeros((RR, 2 * HD), F32)
            for j in range(0, KT, BC):
                x = s_buf[i, r : r + RR, j : j + BC] * scale - high[r : r + RR]
                acc = acc + dot(jnp.exp2(x).astype(BF16), vv[j : j + BC, :])
            accs.append(acc)
        acc = jnp.concatenate(accs, axis=0)
        total = acc[:, HD:]
        out = acc[:, 0:HD] / total
        lse = high + jnp.log2(total)
        lses = [jnp.transpose(lse[r : r + HD]) for r in range(0, NR, HD)]
        row = iota((32, HD), 0)
        for j in range(NS):
            stat = lses[32 * j // HD][0:32, :]
            if 32 * j % HD:
                stat = pltpu.roll(stat, HD - 32 * j % HD, 1)
            first = stat.astype(BF16).astype(F32)
            second = (stat - first).astype(BF16).astype(F32)
            third = stat - first - second
            block = jnp.where(
                row == 14,
                first,
                jnp.where(row == 15, second, jnp.where(row == 30, third, out[32 * j : 32 * j + 32])),
            )
            rs[peers[j]] = block.astype(BF16)
        for j in range(NS):

            if i < n_req // NS - 1 or j < NS - 1:
                pltpu.make_async_remote_copy(
                    src_ref=rs.at[peers[j]],
                    dst_ref=rr.at[me],
                    send_sem=rsend.at[peers[j]],
                    recv_sem=rrecv.at[me],
                    device_id={"req": peers[j]},
                    device_id_type=MESH,
                ).start()

    for i in range(n_req // NS):
        prefix_block(i)
    rr[me] = rs[me]

    load_tk.wait()
    load_tv.wait()

    def tail_scores(c, carry):
        at = pl.ds(pl.multiple_of(c * 16, 16), 16)
        st[at, :] = dot_t(qt[at, :], tk[c])
        return carry

    lax.fori_loop(0, CD, tail_scores, 0, unroll=True)
    tlcol = jnp.sum(
        jnp.where(iota((KR, CD), 1) == iota((KR, CD), 0) // 16, tlen, 0), axis=1, keepdims=True
    )
    mask = iota((KR, TAIL), 1) < tlcol
    s = jnp.where(mask, st[...], NEG)
    m_t = jnp.max(s, axis=1, keepdims=True) * scale
    weights = jnp.where(mask, jnp.exp2(s * scale - m_t), 0.0).astype(BF16).astype(F32)
    l_t = jnp.sum(weights, axis=1, keepdims=True)
    st[...] = weights

    def tail_out(c, carry):
        at = pl.ds(pl.multiple_of(c * 16, 16), 16)
        to[at, :] = dot(st[at, :].astype(BF16), tv[c])
        return carry

    lax.fori_loop(0, CD, tail_out, 0, unroll=True)

    q32 = qt[...].astype(F32)
    hrow = iota((KR, ROWS), 0)
    odd = lax.rem(iota((KR, 1), 0), T) == 1
    pick0 = onehot(iota((KR, ROWS), 1) == (hrow // 16) * T)
    pick1 = onehot(iota((KR, ROWS), 1) == (hrow // 16) * T + 1)
    s0 = jnp.sum(q32 * dot(pick0, key_new), axis=1, keepdims=True) * scale
    s1 = jnp.where(odd, jnp.sum(q32 * dot(pick1, key_new), axis=1, keepdims=True) * scale, NEG)
    m_f = jnp.maximum(s0, s1)
    w0 = jnp.exp2(s0 - m_f).astype(BF16).astype(F32)
    w1 = jnp.where(odd, jnp.exp2(s1 - m_f), 0.0).astype(BF16).astype(F32)
    l_f = w0 + w1
    o_f = w0 * dot(pick0, value_new) + w1 * dot(pick1, value_new)

    lane = iota((KR, n_x), 1)
    inside = lax.rem(lane, 32)
    stat_at = ((inside == 14) | (inside == 15) | (inside == 30)) & (lane // 32 == tcol // 32)
    pick_o[...] = onehot(lane == tcol)
    pick_s[...] = onehot(stat_at)
    brow2 = iota((G * ROWS, KR), 0)
    back = (lax.rem(brow2, ROWS) // T) * 16 + (brow2 // ROWS) * T + lax.rem(brow2, T)
    pick_b[...] = onehot(iota((G * ROWS, KR), 1) == back)
    for k in range(1, n_req):
        src = lax.rem(me + k, n_req)
        pltpu.make_async_remote_copy(
            src_ref=rs.at[src],
            dst_ref=rr.at[src],
            send_sem=rsend.at[src],
            recv_sem=rrecv.at[src],
            device_id={"req": src},
            device_id_type=MESH,
        ).wait_recv()
    parts = jnp.concatenate([rr[p] for p in range(n_req)], axis=0)
    o_p = dot(pick_o[...], parts)
    stats = dot(pick_s[...], parts)
    lse_p = jnp.sum(
        jnp.where(iota((KR, HD), 1) == lax.rem(tcol, 32), stats, 0.0), axis=1, keepdims=True
    )

    top = jnp.maximum(jnp.maximum(lse_p, m_t), m_f)
    f_p = jnp.exp2(lse_p - top)
    f_t = jnp.exp2(m_t - top)
    f_f = jnp.exp2(m_f - top)
    numer = f_p * o_p + f_t * to[...] + f_f * o_f
    denom = f_p + f_t * l_t + f_f * l_f
    attended = (numer / denom).astype(BF16)
    final = dot(pick_b[...], attended)
    partial = jnp.zeros((ROWS, HD), F32)
    for g in range(G):
        x = final[g * ROWS : (g + 1) * ROWS]
        outv[:, g * HD : (g + 1) * HD] = x.astype(BF16)
        partial = partial + x * sw_ref[pl.ds(g * HD, HD)].reshape(1, HD)
    store_out = pltpu.make_async_copy(outv, out_ref, out_sem)
    store_out.start()
    column = jnp.sum(partial, axis=1, keepdims=True)
    line = jnp.sum(
        jnp.where(iota((ROWS, HD), 0) == iota((ROWS, HD), 1) * T + 1, column, 0.0),
        axis=0,
        keepdims=True,
    )
    line = jnp.broadcast_to(line, (8, HD))
    scs[...] = line
    scr[mt] = line

    def score_copy(slot_at, k, dev):
        return pltpu.make_async_remote_copy(
            src_ref=scs,
            dst_ref=scr.at[slot_at],
            send_sem=ssend.at[k],
            recv_sem=srecv.at[slot_at],
            device_id={"tp": dev},
            device_id_type=MESH,
        )

    for k in range(1, n_tp):
        score_copy(mt, k, lax.rem(mt + k, n_tp)).start()
    for k in range(1, n_tp):
        src = lax.rem(mt + k, n_tp)
        score_copy(src, k, src).wait_recv()
    total = scr[0]
    for k in range(1, n_tp):
        total = total + scr[k]
    score_ref[...] = total

    store_out.wait()

    for k in range(1, n_tp):
        dev = lax.rem(mt + k, n_tp)
        score_copy(dev, k, dev).wait_send()
    for k in range(1, n_req):
        dev = lax.rem(me + k, n_req)
        query_copy(dev, dev).wait_send()
        pltpu.make_async_remote_copy(
            src_ref=rs.at[dev],
            dst_ref=rr.at[me],
            send_sem=rsend.at[dev],
            recv_sem=rrecv.at[me],
            device_id={"req": dev},
            device_id_type=MESH,
        ).wait_send()


def finish(rows_ref, line_ref, out_ref, score_ref):
    CD, T = out_ref.shape[:2]
    for c in range(CD):
        out_ref[c] = rows_ref[c * T : (c + 1) * T, :]
    score_ref[...] = line_ref[0, 0:CD]


def per_device(
    inner,
    n_req,
    n_tp,
    new_hidden,
    norm_gain,
    w_query,
    w_key,
    w_value,
    hidden_store,
    key_cache,
    value_cache,
    tail_keys,
    tail_values,
    prompt_len,
    tail_len,
    recomp_pos,
    cont_prompt,
    score_weight,
):
    CD, T, D = new_hidden.shape
    QW = w_query.shape[1]
    G = QW // HD
    CTX = key_cache.shape[1]
    TAIL = tail_keys.shape[1]
    RECOMP = hidden_store.shape[1]
    ROWS = CD * T
    RP = -(-RECOMP // 32) * 32
    NB = -(-RECOMP // HD) * HD
    KT = CTX + 512
    CH = 512
    KR = CD * 16
    NR = 2 * inner * 32
    half = HD // 2
    freq = THETA ** (-2.0 * np.arange(half, dtype=np.float64) / HD)
    freq = np.concatenate([freq, freq]).astype(np.float32)[None, :]
    dims = (n_req, n_tp, inner, D, CTX, TAIL, RECOMP, CD, G)
    hbm = pl.BlockSpec(memory_space=pl.ANY)
    vmem = pl.BlockSpec(memory_space=pltpu.VMEM)
    dma = pltpu.SemaphoreType.DMA
    attended, scores = pl.pallas_call(
        functools.partial(kernel, dims),
        out_shape=(
            jax.ShapeDtypeStruct((ROWS, QW), BF16),
            jax.ShapeDtypeStruct((8, HD), F32),
        ),
        in_specs=[hbm] * 16,
        out_specs=(hbm, vmem),
        scratch_shapes=[
            pltpu.VMEM((ROWS, D), BF16),
            pltpu.VMEM((1, D), F32),
            pltpu.VMEM((1, prompt_len.shape[0]), I32),
            pltpu.VMEM((1, CD), I32),
            pltpu.VMEM((1, RECOMP), I32),
            pltpu.VMEM((1, cont_prompt.shape[0]), I32),
            pltpu.VMEM((QW,), F32),
            pltpu.VMEM((1, HD), F32),
            pltpu.VMEM((D // CH, CH, QW), BF16),
            pltpu.VMEM((D, 2 * HD), BF16),
            pltpu.VMEM((RECOMP, D), BF16),
            pltpu.VMEM((RP + ROWS, D), BF16),
            pltpu.VMEM((KT, HD), BF16),
            pltpu.VMEM((KT, 2 * HD), BF16),
            pltpu.VMEM((CD, TAIL, HD), BF16),
            pltpu.VMEM((CD, TAIL, HD), BF16),
            pltpu.VMEM((1, NB), I32),
            pltpu.VMEM((NB, HD), F32),
            pltpu.VMEM((RP, HD), F32),
            pltpu.VMEM((RP, HD), F32),
            pltpu.VMEM((1, KT), F32),
            pltpu.VMEM((ROWS, QW), F32),
            pltpu.VMEM((RP + ROWS, 2 * HD), F32),
            pltpu.VMEM((G * ROWS, HD), BF16),
            pltpu.VMEM((KR, HD), BF16),
            pltpu.VMEM((n_req, 32, HD), BF16),
            pltpu.VMEM((n_req, 32, HD), BF16),
            pltpu.VMEM((n_req * 32 // NR, NR, KT), F32),
            pltpu.VMEM((n_req, 32, HD), BF16),
            pltpu.VMEM((n_req, 32, HD), BF16),
            pltpu.VMEM((KR, TAIL), F32),
            pltpu.VMEM((KR, HD), F32),
            pltpu.VMEM((8, HD), F32),
            pltpu.VMEM((n_tp, 8, HD), F32),
            pltpu.VMEM((KR, n_req * 32), BF16),
            pltpu.VMEM((KR, n_req * 32), BF16),
            pltpu.VMEM((G * ROWS, KR), BF16),
            pltpu.VMEM((ROWS, QW), BF16),
            dma,
            dma((15,)),
            dma((CD,)),
            dma((D // CH,)),
            dma((n_req,)),
            dma((n_req,)),
            dma((n_req,)),
            dma((n_req,)),
            dma((n_tp,)),
            dma((n_tp,)),
        ],
        compiler_params=pltpu.CompilerParams(
            collective_id=0, has_side_effects=True, vmem_limit_bytes=67_043_328
        ),
        name="decode",
    )(
        new_hidden,
        norm_gain.reshape(1, D),
        w_query,
        w_key,
        w_value,
        hidden_store,
        key_cache,
        value_cache,
        tail_keys,
        tail_values,
        prompt_len.reshape(1, -1),
        tail_len.reshape(1, -1),
        recomp_pos,
        cont_prompt.reshape(1, -1),
        score_weight,
        jnp.asarray(freq),
    )
    return pl.pallas_call(
        finish,
        out_shape=(
            jax.ShapeDtypeStruct((CD, T, QW), BF16),
            jax.ShapeDtypeStruct((CD,), F32),
        ),
        in_specs=[vmem, vmem],
        out_specs=(vmem, vmem),
        compiler_params=pltpu.CompilerParams(vmem_limit_bytes=67_043_328),
        name="finish",
    )(attended, scores)


def solution(mesh):
    placed = (
        P("req", None, None),
        P(),
        P(None, "tp"),
        P(None, "tp"),
        P(None, "tp"),
        P("req", None, None),
        P("req", None, "tp"),
        P("req", None, "tp"),
        P("req", None, "tp"),
        P("req", None, "tp"),
        P(),
        P("req"),
        P("req", None),
        P(),
        P("tp"),
    )
    n_req = mesh.shape["req"]
    inner = 4 if n_req % 4 == 0 else 1
    return jax.shard_map(
        functools.partial(per_device, inner, n_req, mesh.shape["tp"]),
        mesh=mesh,
        in_specs=placed,
        out_specs=(P("req", None, "tp"), P("req")),
        check_vma=False,
    )
```

```python
import functools
import math

import jax
import jax.numpy as jnp
import numpy as np
from jax import lax
from jax.experimental import pallas as pl
from jax.experimental.pallas import tpu as pltpu
from jax.sharding import PartitionSpec as P

MESH = pl.DeviceIdType.MESH
HD = 128
NEG = -1e30
THETA = 5000000.0
LOG2E = math.log2(math.e)
F32 = jnp.float32
BF16 = jnp.bfloat16
I32 = jnp.int32


def iota(shape, dim):
    return lax.broadcasted_iota(I32, shape, dim)


def dot(a, b):
    return jnp.dot(a, b, preferred_element_type=F32)


def dot_t(a, b):
    return lax.dot_general(a, b, (((1,), (1,)), ((), ())), preferred_element_type=F32)


def onehot(mask):
    return jnp.where(mask, 1.0, 0.0).astype(BF16)


def kernel(
    dims,
    nh_hbm,
    gain_hbm,
    wq_hbm,
    wk_hbm,
    wv_hbm,
    hs_hbm,
    kc_hbm,
    vc_hbm,
    tk_hbm,
    tv_hbm,
    plen_hbm,
    tlen_hbm,
    rpos_hbm,
    cont_hbm,
    sw_hbm,
    freq_hbm,
    out_ref,
    score_ref,
    nh,
    gain_ref,
    plen_ref,
    tlen_ref,
    rpos_ref,
    cont_ref,
    sw_ref,
    freq_ref,
    wq,
    w,
    hs,
    sn,
    kk,
    vv,
    tk,
    tv,
    pos_row,
    posb,
    ropec,
    ropes,
    bias,
    qacc,
    kvacc,
    qs,
    qt,
    xs,
    rq,
    s_buf,
    rs,
    rr,
    st,
    to,
    scs,
    scr,
    pick_o,
    pick_s,
    pick_b,
    outv,
    out_sem,
    in_sem,
    nh_sem,
    wq_sem,
    qsend,
    qrecv,
    rsend,
    rrecv,
    ssend,
    srecv,
):
    n_req, n_tp, inner, D, CTX, TAIL, RECOMP, CD, G = dims
    T = 2
    ROWS = CD * T
    RP = -(-RECOMP // 32) * 32
    KT = kk.shape[0]
    outer = n_req // inner
    me = lax.axis_index("req")
    mt = lax.axis_index("tp")
    scale = HD ** (-0.5) * LOG2E
    CH = wq.shape[1]
    n_ch = wq.shape[0]

    loads_nh = [
        pltpu.make_async_copy(nh_hbm.at[c], nh.at[pl.ds(c * T, T)], nh_sem.at[c]) for c in range(CD)
    ]
    for copy in loads_nh:
        copy.start()
    small = (
        (gain_hbm, gain_ref),
        (plen_hbm, plen_ref),
        (tlen_hbm, tlen_ref),
        (rpos_hbm, rpos_ref),
        (cont_hbm, cont_ref),
        (sw_hbm, sw_ref),
        (freq_hbm, freq_ref),
    )
    loads_small = [
        pltpu.make_async_copy(src, dst, in_sem.at[8 + i]) for i, (src, dst) in enumerate(small)
    ]
    for copy in loads_small:
        copy.start()
    loads_q = [
        pltpu.make_async_copy(wq_hbm.at[pl.ds(i * CH, CH)], wq.at[i], wq_sem.at[i])
        for i in range(n_ch)
    ]
    DEPTH = min(6, n_ch)
    for copy in loads_q[:DEPTH]:
        copy.start()
    load_wk = pltpu.make_async_copy(wk_hbm, w.at[:, pl.ds(0, HD)], in_sem.at[1])
    load_wv = pltpu.make_async_copy(wv_hbm, w.at[:, pl.ds(HD, HD)], in_sem.at[2])
    load_hs = pltpu.make_async_copy(hs_hbm.at[0], hs, in_sem.at[3])
    load_kc = pltpu.make_async_copy(kc_hbm.at[0], kk.at[pl.ds(0, CTX)], in_sem.at[4])
    load_vc = pltpu.make_async_copy(
        vc_hbm.at[0], vv.at[pl.ds(0, CTX), pl.ds(0, HD)], in_sem.at[5]
    )
    load_tk = pltpu.make_async_copy(tk_hbm, tk, in_sem.at[6])
    load_tv = pltpu.make_async_copy(tv_hbm, tv, in_sem.at[7])
    after = loads_q[DEPTH:] + [load_hs, load_wk, load_wv, load_kc, load_vc, load_tk, load_tv]

    barrier = pltpu.get_barrier_semaphore()
    for k in range(1, n_req):
        pl.semaphore_signal(
            barrier, inc=1, device_id={"req": lax.rem(me + k, n_req)}, device_id_type=MESH
        )
    for k in range(1, n_tp):
        pl.semaphore_signal(
            barrier, inc=1, device_id={"tp": lax.rem(mt + k, n_tp)}, device_id_type=MESH
        )

    vv[:, HD:] = jnp.ones((KT, HD), BF16)
    kk[CTX:, :] = jnp.zeros((KT - CTX, HD), BF16)
    vv[CTX:, 0:HD] = jnp.zeros((KT - CTX, HD), BF16)

    for copy in loads_small:
        copy.wait()

    def norm_block(load, store):
        total = None
        for j in range(0, D, 512):
            x = load(j).astype(F32)
            x = x * x
            for i in range(0, 512, HD):
                total = x[:, i : i + HD] if total is None else total + x[:, i : i + HD]
        factor = lax.rsqrt(jnp.sum(total, axis=1, keepdims=True) * (1.0 / D) + 1e-05)
        for j in range(0, D, 512):
            x = load(j).astype(F32)
            store(j, x * factor * gain_ref[:, j : j + 512])

    for copy in loads_nh:
        copy.wait()
    for r in range(0, ROWS, ROWS):

        def load_new(j, r=r):
            return nh[r : r + ROWS, j : j + 512]

        def store_new(j, x, r=r):
            sn[RP + r : RP + r + ROWS, j : j + 512] = x.astype(BF16)

        norm_block(load_new, store_new)

    for i in range(n_ch):
        loads_q[i].wait()
        for copy in after[i : i + 1] if i < n_ch - 1 else after[i:]:
            copy.start()
        part = dot(sn[RP : RP + ROWS, i * CH : (i + 1) * CH], wq[i])
        if i == 0:
            qacc[...] = part
        else:
            qacc[...] += part
    crow = cont_ref[...]
    pcol = jnp.sum(
        jnp.where(iota((CD, crow.shape[1]), 1) == me * CD + iota((CD, crow.shape[1]), 0), crow, 0),
        axis=1,
        keepdims=True,
    )
    eye = iota((CD, HD), 0) == iota((CD, HD), 1)
    prow = jnp.sum(jnp.where(eye, pcol, 0), axis=0, keepdims=True)
    earlier = (prow == pcol) & (iota((CD, HD), 1) < iota((CD, HD), 0))
    slot = jnp.sum(jnp.where(earlier, 1, 0), axis=1, keepdims=True)
    base = pcol * 32 + slot * 16
    KR = CD * 16
    QR = G * ROWS
    qcol = iota((1, QR), 1)
    trow = jnp.sum(
        jnp.where(iota((CD, QR), 0) == lax.rem(iota((CD, QR), 1), ROWS) // T, base, 0),
        axis=0,
        keepdims=True,
    ) + (qcol // ROWS * T + lax.rem(qcol, T))
    brow = jnp.sum(jnp.where(eye, base, 0), axis=0, keepdims=True)
    own = iota((KR, HD), 1) == iota((KR, HD), 0) // 16
    tcol = jnp.sum(jnp.where(own, brow, 0), axis=1, keepdims=True) + lax.rem(
        iota((KR, 1), 0), 16
    )

    n_p = plen_ref.shape[1]
    plen = plen_ref[...]
    tlen = tlen_ref[...]
    clen = jnp.sum(
        jnp.where(iota((CD, n_p), 1) == pcol, plen, 0), axis=1, keepdims=True
    ) + jnp.sum(jnp.where(iota((CD, CD), 0) == iota((CD, CD), 1), tlen, 0), axis=1, keepdims=True)
    lrow = jnp.sum(jnp.where(eye, clen, 0), axis=0, keepdims=True)
    pos_new = jnp.sum(
        jnp.where(iota((ROWS, HD), 1) == iota((ROWS, HD), 0) // T, lrow, 0), axis=1, keepdims=True
    ) + lax.rem(iota((ROWS, 1), 0), T)
    freq = freq_ref[...]
    sign = jnp.where(iota((1, HD), 1) < HD // 2, -1.0, 1.0)
    angle = pos_new.astype(F32) * freq
    cos_new = jnp.cos(angle)
    sin_new = jnp.sin(angle) * sign

    for g in range(G):
        x = qacc[:, g * HD : (g + 1) * HD]
        x = x * cos_new + pltpu.roll(x, HD // 2, 1) * sin_new
        qs[g * ROWS : (g + 1) * ROWS, :] = x.astype(BF16)
    n_x = n_req * 32
    sent = dot(onehot(iota((n_x, QR), 0) == trow), qs[...]).astype(BF16)
    for p in range(n_req):
        xs[p] = sent[p * 32 : (p + 1) * 32]

    pl.semaphore_wait(barrier, n_req + n_tp - 2)

    def peer(k):
        z = lax.rem(me // inner + k // inner, outer)
        y = lax.rem(lax.rem(me, inner) + lax.rem(k, inner), inner)
        return z * inner + y

    def query_copy(slot_at, to_dev):
        return pltpu.make_async_remote_copy(
            src_ref=xs.at[slot_at],
            dst_ref=rq.at[me],
            send_sem=qsend.at[slot_at],
            recv_sem=qrecv.at[me],
            device_id={"req": to_dev},
            device_id_type=MESH,
        )

    def query_arrival(src):
        return pltpu.make_async_remote_copy(
            src_ref=xs.at[src],
            dst_ref=rq.at[src],
            send_sem=qsend.at[src],
            recv_sem=qrecv.at[src],
            device_id={"req": src},
            device_id_type=MESH,
        )

    for k in range(1, n_req):
        to_dev = lax.rem(me + k, n_req)
        query_copy(to_dev, to_dev).start()
    rq[me] = xs[me]
    krow = iota((KR, G * ROWS), 0)
    picks = (lax.rem(krow, 16) // T) * ROWS + (krow // 16) * T + lax.rem(krow, T)
    qt[...] = dot(onehot(iota((KR, G * ROWS), 1) == picks), qs[...]).astype(BF16)

    NB = posb.shape[0]
    pos_row[...] = jnp.full(pos_row.shape, -1, I32)
    pos_row[:, 0:RECOMP] = rpos_ref[...]
    for j in range(0, NB, HD):
        chunk = pos_row[:, j : j + HD].astype(F32)
        posb[j : j + HD, :] = jnp.transpose(jnp.broadcast_to(chunk, (HD, HD)))

    TB = RP // 4

    def tables(i, carry):
        at = pl.ds(pl.multiple_of(i * TB, 8), TB)
        turned = posb[at, :] * freq
        ropec[at, :] = jnp.cos(turned)
        ropes[at, :] = jnp.sin(turned) * sign
        return carry

    lax.fori_loop(0, RP // TB, tables, 0)
    my_len = jnp.sum(jnp.where(iota((1, n_p), 1) == me, plen, 0), axis=1, keepdims=True).astype(F32)
    for b in range(0, CTX, HD):
        first = b // 10 // 8 * 8
        rows = min(24, NB - first)
        here = (b + iota((1, HD), 1)).astype(F32)
        same = jnp.where(posb[first : first + rows, :] == here, 1.0, 0.0)
        replaced = jnp.max(same, axis=0, keepdims=True)
        bias[:, b : b + HD] = jnp.where((replaced > 0.0) | (here >= my_len), NEG, 0.0)
    for b in range(0, KT - CTX, HD):
        if b < NB:
            at = pos_row[:, b : b + HD].astype(F32)
            bias[:, CTX + b : CTX + b + HD] = jnp.where((at < 0.0) | (at >= my_len), NEG, 0.0)
        else:
            bias[:, CTX + b : CTX + b + HD] = jnp.full((1, HD), NEG, F32)

    load_hs.wait()

    NB_ROWS = 80 if RECOMP >= 80 else 16

    def stored_block(i, carry):
        at = pl.ds(pl.multiple_of(i * NB_ROWS, 16), NB_ROWS)

        def load_old(j):
            return hs[at, j : j + 512]

        def store_old(j, x):
            sn[at, j : j + 512] = x.astype(BF16)

        norm_block(load_old, store_old)
        return carry

    lax.fori_loop(0, RECOMP // NB_ROWS, stored_block, 0)
    if RECOMP < RP:
        last = RECOMP // NB_ROWS * NB_ROWS
        sn[last:RP, :] = jnp.zeros((RP - last, D), BF16)
        if last < RECOMP:

            def load_last(j):
                return hs[last:RECOMP, j : j + 512]

            def store_last(j, x):
                sn[last:RECOMP, j : j + 512] = x.astype(BF16)

            norm_block(load_last, store_last)
    load_wk.wait()
    load_wv.wait()
    KC = D // 4
    kvacc[...] = dot(sn[:, 0:KC], w[0:KC, :])

    def kv_chunk(i, carry):
        at = pl.ds(pl.multiple_of(i * KC, HD), KC)
        kvacc[...] += dot(sn[:, at], w[at, :])
        return carry

    lax.fori_loop(1, 4, kv_chunk, 0)
    x = kvacc[0:RP, 0:HD]
    x = x * ropec[0:RP, :] + pltpu.roll(x, HD // 2, 1) * ropes[0:RP, :]
    load_kc.wait()
    load_vc.wait()
    kk[CTX : CTX + RP, :] = x.astype(BF16)
    vv[CTX : CTX + RP, 0:HD] = kvacc[0:RP, HD:].astype(BF16)
    x = kvacc[RP : RP + ROWS, 0:HD]
    key_new = (x * cos_new + pltpu.roll(x, HD // 2, 1) * sin_new).astype(BF16)
    value_new = kvacc[RP : RP + ROWS, HD:].astype(BF16)

    BC = 256
    RR = HD
    NS = 2 * inner
    NR = NS * 32

    def prefix_block(i):
        peers = [peer(n_req - 1 - i * NS - j) for j in range(NS)]
        for j in range(NS):

            if i < n_req // NS - 1 or j < NS - 1:
                query_arrival(peers[j]).wait_recv()

        q = jnp.concatenate([rq[p] for p in peers], axis=0)
        top = None
        for j in range(0, KT, BC):
            s = dot_t(q, kk[j : j + BC, :]) + bias[:, j : j + BC]
            s_buf[i, :, j : j + BC] = s
            for b in range(0, BC, HD):
                part = s[:, b : b + HD]
                top = part if top is None else jnp.maximum(top, part)
        high = jnp.max(top, axis=1, keepdims=True) * scale
        accs = []
        for r in range(0, NR, RR):
            acc = jnp.zeros((RR, 2 * HD), F32)
            for j in range(0, KT, BC):
                x = s_buf[i, r : r + RR, j : j + BC] * scale - high[r : r + RR]
                acc = acc + dot(jnp.exp2(x).astype(BF16), vv[j : j + BC, :])
            accs.append(acc)
        acc = jnp.concatenate(accs, axis=0)
        total = acc[:, HD:]
        out = acc[:, 0:HD] / total
        lse = high + jnp.log2(total)
        lses = [jnp.transpose(lse[r : r + HD]) for r in range(0, NR, HD)]
        row = iota((32, HD), 0)
        for j in range(NS):
            stat = lses[32 * j // HD][0:32, :]
            if 32 * j % HD:
                stat = pltpu.roll(stat, HD - 32 * j % HD, 1)
            first = stat.astype(BF16).astype(F32)
            second = (stat - first).astype(BF16).astype(F32)
            third = stat - first - second
            block = jnp.where(
                row == 14,
                first,
                jnp.where(row == 15, second, jnp.where(row == 30, third, out[32 * j : 32 * j + 32])),
            )
            rs[peers[j]] = block.astype(BF16)
        for j in range(NS):

            if i < n_req // NS - 1 or j < NS - 1:
                pltpu.make_async_remote_copy(
                    src_ref=rs.at[peers[j]],
                    dst_ref=rr.at[me],
                    send_sem=rsend.at[peers[j]],
                    recv_sem=rrecv.at[me],
                    device_id={"req": peers[j]},
                    device_id_type=MESH,
                ).start()

    for i in range(n_req // NS):
        prefix_block(i)
    rr[me] = rs[me]

    load_tk.wait()
    load_tv.wait()

    def tail_scores(c, carry):
        at = pl.ds(pl.multiple_of(c * 16, 16), 16)
        st[at, :] = dot_t(qt[at, :], tk[c])
        return carry

    lax.fori_loop(0, CD, tail_scores, 0, unroll=True)
    tlcol = jnp.sum(
        jnp.where(iota((KR, CD), 1) == iota((KR, CD), 0) // 16, tlen, 0), axis=1, keepdims=True
    )
    mask = iota((KR, TAIL), 1) < tlcol
    s = jnp.where(mask, st[...], NEG)
    m_t = jnp.max(s, axis=1, keepdims=True) * scale
    weights = jnp.where(mask, jnp.exp2(s * scale - m_t), 0.0).astype(BF16).astype(F32)
    l_t = jnp.sum(weights, axis=1, keepdims=True)
    st[...] = weights

    def tail_out(c, carry):
        at = pl.ds(pl.multiple_of(c * 16, 16), 16)
        to[at, :] = dot(st[at, :].astype(BF16), tv[c])
        return carry

    lax.fori_loop(0, CD, tail_out, 0, unroll=True)

    q32 = qt[...].astype(F32)
    hrow = iota((KR, ROWS), 0)
    odd = lax.rem(iota((KR, 1), 0), T) == 1
    pick0 = onehot(iota((KR, ROWS), 1) == (hrow // 16) * T)
    pick1 = onehot(iota((KR, ROWS), 1) == (hrow // 16) * T + 1)
    s0 = jnp.sum(q32 * dot(pick0, key_new), axis=1, keepdims=True) * scale
    s1 = jnp.where(odd, jnp.sum(q32 * dot(pick1, key_new), axis=1, keepdims=True) * scale, NEG)
    m_f = jnp.maximum(s0, s1)
    w0 = jnp.exp2(s0 - m_f).astype(BF16).astype(F32)
    w1 = jnp.where(odd, jnp.exp2(s1 - m_f), 0.0).astype(BF16).astype(F32)
    l_f = w0 + w1
    o_f = w0 * dot(pick0, value_new) + w1 * dot(pick1, value_new)

    lane = iota((KR, n_x), 1)
    inside = lax.rem(lane, 32)
    stat_at = ((inside == 14) | (inside == 15) | (inside == 30)) & (lane // 32 == tcol // 32)
    pick_o[...] = onehot(lane == tcol)
    pick_s[...] = onehot(stat_at)
    brow2 = iota((G * ROWS, KR), 0)
    back = (lax.rem(brow2, ROWS) // T) * 16 + (brow2 // ROWS) * T + lax.rem(brow2, T)
    pick_b[...] = onehot(iota((G * ROWS, KR), 1) == back)
    for k in range(1, n_req):
        src = lax.rem(me + k, n_req)
        pltpu.make_async_remote_copy(
            src_ref=rs.at[src],
            dst_ref=rr.at[src],
            send_sem=rsend.at[src],
            recv_sem=rrecv.at[src],
            device_id={"req": src},
            device_id_type=MESH,
        ).wait_recv()
    parts = jnp.concatenate([rr[p] for p in range(n_req)], axis=0)
    o_p = dot(pick_o[...], parts)
    stats = dot(pick_s[...], parts)
    lse_p = jnp.sum(
        jnp.where(iota((KR, HD), 1) == lax.rem(tcol, 32), stats, 0.0), axis=1, keepdims=True
    )

    top = jnp.maximum(jnp.maximum(lse_p, m_t), m_f)
    f_p = jnp.exp2(lse_p - top)
    f_t = jnp.exp2(m_t - top)
    f_f = jnp.exp2(m_f - top)
    numer = f_p * o_p + f_t * to[...] + f_f * o_f
    denom = f_p + f_t * l_t + f_f * l_f
    attended = (numer / denom).astype(BF16)
    final = dot(pick_b[...], attended)
    partial = jnp.zeros((ROWS, HD), F32)
    for g in range(G):
        x = final[g * ROWS : (g + 1) * ROWS]
        outv[:, g * HD : (g + 1) * HD] = x.astype(BF16)
        partial = partial + x * sw_ref[pl.ds(g * HD, HD)].reshape(1, HD)
    store_out = pltpu.make_async_copy(outv, out_ref, out_sem)
    store_out.start()
    column = jnp.sum(partial, axis=1, keepdims=True)
    line = jnp.sum(
        jnp.where(iota((ROWS, HD), 0) == iota((ROWS, HD), 1) * T + 1, column, 0.0),
        axis=0,
        keepdims=True,
    )
    line = jnp.broadcast_to(line, (8, HD))
    scs[...] = line
    scr[mt] = line

    def score_copy(slot_at, k, dev):
        return pltpu.make_async_remote_copy(
            src_ref=scs,
            dst_ref=scr.at[slot_at],
            send_sem=ssend.at[k],
            recv_sem=srecv.at[slot_at],
            device_id={"tp": dev},
            device_id_type=MESH,
        )

    for k in range(1, n_tp):
        score_copy(mt, k, lax.rem(mt + k, n_tp)).start()
    for k in range(1, n_tp):
        src = lax.rem(mt + k, n_tp)
        score_copy(src, k, src).wait_recv()
    total = scr[0]
    for k in range(1, n_tp):
        total = total + scr[k]
    score_ref[...] = total

    store_out.wait()

    for k in range(1, n_tp):
        dev = lax.rem(mt + k, n_tp)
        score_copy(dev, k, dev).wait_send()
    for k in range(1, n_req):
        dev = lax.rem(me + k, n_req)
        query_copy(dev, dev).wait_send()
        pltpu.make_async_remote_copy(
            src_ref=rs.at[dev],
            dst_ref=rr.at[me],
            send_sem=rsend.at[dev],
            recv_sem=rrecv.at[me],
            device_id={"req": dev},
            device_id_type=MESH,
        ).wait_send()


def finish(rows_ref, line_ref, out_ref, score_ref):
    CD, T = out_ref.shape[:2]
    for c in range(CD):
        out_ref[c] = rows_ref[c * T : (c + 1) * T, :]
    score_ref[...] = line_ref[0, 0:CD]


def per_device(
    inner,
    n_req,
    n_tp,
    new_hidden,
    norm_gain,
    w_query,
    w_key,
    w_value,
    hidden_store,
    key_cache,
    value_cache,
    tail_keys,
    tail_values,
    prompt_len,
    tail_len,
    recomp_pos,
    cont_prompt,
    score_weight,
):
    CD, T, D = new_hidden.shape
    QW = w_query.shape[1]
    G = QW // HD
    CTX = key_cache.shape[1]
    TAIL = tail_keys.shape[1]
    RECOMP = hidden_store.shape[1]
    ROWS = CD * T
    RP = -(-RECOMP // 32) * 32
    NB = -(-RECOMP // HD) * HD
    KT = CTX + 512
    CH = 512
    KR = CD * 16
    NR = 2 * inner * 32
    half = HD // 2
    freq = THETA ** (-2.0 * np.arange(half, dtype=np.float64) / HD)
    freq = np.concatenate([freq, freq]).astype(np.float32)[None, :]
    dims = (n_req, n_tp, inner, D, CTX, TAIL, RECOMP, CD, G)
    hbm = pl.BlockSpec(memory_space=pl.ANY)
    vmem = pl.BlockSpec(memory_space=pltpu.VMEM)
    dma = pltpu.SemaphoreType.DMA
    attended, scores = pl.pallas_call(
        functools.partial(kernel, dims),
        out_shape=(
            jax.ShapeDtypeStruct((ROWS, QW), BF16),
            jax.ShapeDtypeStruct((8, HD), F32),
        ),
        in_specs=[hbm] * 16,
        out_specs=(hbm, vmem),
        scratch_shapes=[
            pltpu.VMEM((ROWS, D), BF16),
            pltpu.VMEM((1, D), F32),
            pltpu.VMEM((1, prompt_len.shape[0]), I32),
            pltpu.VMEM((1, CD), I32),
            pltpu.VMEM((1, RECOMP), I32),
            pltpu.VMEM((1, cont_prompt.shape[0]), I32),
            pltpu.VMEM((QW,), F32),
            pltpu.VMEM((1, HD), F32),
            pltpu.VMEM((D // CH, CH, QW), BF16),
            pltpu.VMEM((D, 2 * HD), BF16),
            pltpu.VMEM((RECOMP, D), BF16),
            pltpu.VMEM((RP + ROWS, D), BF16),
            pltpu.VMEM((KT, HD), BF16),
            pltpu.VMEM((KT, 2 * HD), BF16),
            pltpu.VMEM((CD, TAIL, HD), BF16),
            pltpu.VMEM((CD, TAIL, HD), BF16),
            pltpu.VMEM((1, NB), I32),
            pltpu.VMEM((NB, HD), F32),
            pltpu.VMEM((RP, HD), F32),
            pltpu.VMEM((RP, HD), F32),
            pltpu.VMEM((1, KT), F32),
            pltpu.VMEM((ROWS, QW), F32),
            pltpu.VMEM((RP + ROWS, 2 * HD), F32),
            pltpu.VMEM((G * ROWS, HD), BF16),
            pltpu.VMEM((KR, HD), BF16),
            pltpu.VMEM((n_req, 32, HD), BF16),
            pltpu.VMEM((n_req, 32, HD), BF16),
            pltpu.VMEM((n_req * 32 // NR, NR, KT), F32),
            pltpu.VMEM((n_req, 32, HD), BF16),
            pltpu.VMEM((n_req, 32, HD), BF16),
            pltpu.VMEM((KR, TAIL), F32),
            pltpu.VMEM((KR, HD), F32),
            pltpu.VMEM((8, HD), F32),
            pltpu.VMEM((n_tp, 8, HD), F32),
            pltpu.VMEM((KR, n_req * 32), BF16),
            pltpu.VMEM((KR, n_req * 32), BF16),
            pltpu.VMEM((G * ROWS, KR), BF16),
            pltpu.VMEM((ROWS, QW), BF16),
            dma,
            dma((15,)),
            dma((CD,)),
            dma((D // CH,)),
            dma((n_req,)),
            dma((n_req,)),
            dma((n_req,)),
            dma((n_req,)),
            dma((n_tp,)),
            dma((n_tp,)),
        ],
        compiler_params=pltpu.CompilerParams(
            collective_id=0, has_side_effects=True, vmem_limit_bytes=67_043_328
        ),
        name="decode",
    )(
        new_hidden,
        norm_gain.reshape(1, D),
        w_query,
        w_key,
        w_value,
        hidden_store,
        key_cache,
        value_cache,
        tail_keys,
        tail_values,
        prompt_len.reshape(1, -1),
        tail_len.reshape(1, -1),
        recomp_pos,
        cont_prompt.reshape(1, -1),
        score_weight,
        jnp.asarray(freq),
    )
    return pl.pallas_call(
        finish,
        out_shape=(
            jax.ShapeDtypeStruct((CD, T, QW), BF16),
            jax.ShapeDtypeStruct((CD,), F32),
        ),
        in_specs=[vmem, vmem],
        out_specs=(vmem, vmem),
        compiler_params=pltpu.CompilerParams(vmem_limit_bytes=67_043_328),
        name="finish",
    )(attended, scores)


def solution(mesh):
    placed = (
        P("req", None, None),
        P(),
        P(None, "tp"),
        P(None, "tp"),
        P(None, "tp"),
        P("req", None, None),
        P("req", None, "tp"),
        P("req", None, "tp"),
        P("req", None, "tp"),
        P("req", None, "tp"),
        P(),
        P("req"),
        P("req", None),
        P(),
        P("tp"),
    )
    n_req = mesh.shape["req"]
    inner = 4 if n_req % 4 == 0 else 1
    return jax.shard_map(
        functools.partial(per_device, inner, n_req, mesh.shape["tp"]),
        mesh=mesh,
        in_specs=placed,
        out_specs=(P("req", None, "tp"), P("req")),
        check_vma=False,
    )
```
